256 devices in a mesh: context: 8 (over y, x_lo), tensor: 8 (over z), fsdp: 4 (over x_hi, core).
Axes of the slice: x: 4 (x_hi: 2, x_lo: 2; x = x_hi * 2 + x_lo), y: 4, z: 8, core: 2. Of those that a mesh axis runs over, the one named last changes fastest.
Arguments:
- queries: bfloat16 [4, 1024, 4096], P('fsdp', 'context', 'tensor'), may hold values from -8 to 8
- keys: bfloat16 [4, 1024, 4096], P('fsdp', 'context', 'tensor'), may hold values from -8 to 8
- values: bfloat16 [4, 1024, 4096], P('fsdp', 'context', 'tensor'), may hold values from -6 to 6
- out_grad: bfloat16 [4, 1024, 4096], P('fsdp', 'context', 'tensor'), may hold values from -6 to 6
- out_weight: bfloat16 [4096, 4096], P('fsdp', 'tensor'), may hold values from -0.09375 to 0.09375
- slopes: float32 [32], P('tensor'), may hold values from 0.00012207031 to 0.05
- counts: int32 [4, 8], P('fsdp', 'context'), may hold values from 1 to 128, 640 in all within a row
- gaps: int32 [4, 1024], P('fsdp', 'context'), may hold values from 1 to 12
Outputs:
- query_grad: bfloat16 [4, 1024, 4096], P('fsdp', 'context', 'tensor')
- key_grad: bfloat16 [4, 1024, 4096], P('fsdp', 'context', 'tensor')
- value_grad: bfloat16 [4, 1024, 4096], P('fsdp', 'context', 'tensor')
- weight_grad: float32 [4096, 4096], P('fsdp', 'tensor')
The draws below stay inside these ranges and needn't reach their ends.
Inputs may be any that keep to these rules, and one draw needn't show every extreme that they name: In each sequence the counts sum to 640 and the largest is 128.
All inputs are finite; a program needn't handle non-finite values. No bound on the sum of `counts` on one device may be relied on, other than what follows from the above.
Results may differ from the reference program's by a relative error of at most 0.022.
Values may be sent and summed in bfloat16 or wider, within the bound.
A program may use at most 64 MiB of HBM per device.

```python
import math
import jax
import jax.numpy as jnp
import numpy as np
from jax import lax

D = 4096
HEADS = 32
HEAD_DIM = 128
ROWS = 128
POSITIONS = 1024
SEQS = 4
BOUNDARIES = 640
N_CONTEXT = 8


def fresh_rows(key, salt):
    return jax.random.truncated_normal(jax.random.fold_in(key, salt), -4.0, 4.0, (SEQS, POSITIONS, HEADS * HEAD_DIM), jnp.float32)


def draw_queries(key, part):
    fresh = fresh_rows(key, 1)
    return fresh.astype(jnp.bfloat16)


def draw_keys(key, part):
    fresh = fresh_rows(key, 2)
    return fresh.astype(jnp.bfloat16)


def place_ends(array, stream_key, low, high):
    longest = array.shape.index(max(array.shape))
    spots = []
    for shift in (0, 1):
        where = [jax.random.randint(jax.random.fold_in(stream_key, axis), (), 0, length) for axis, length in enumerate(array.shape)]
        where[longest] = (where[longest] + shift) % array.shape[longest]
        spots.append(tuple(where))
    return array.at[spots[0]].set(low).at[spots[1]].set(high)


def level_of(rng, shape, shards, smallest, largest):
    level, own = 1.0, jax.random.fold_in(rng, 6)
    for axis_at, shards_of in shards:
        heights = jnp.exp(jax.random.uniform(jax.random.fold_in(own, axis_at), (shards_of,), jnp.float32, smallest / len(shards), largest / len(shards)))
        level = level * jnp.repeat(heights, shape[axis_at] // shards_of).reshape([-1 if axis == axis_at else 1 for axis in range(len(shape))])
    return level


def split_up(amount, total, limit, skew):
    weights = [(1 << 20) // math.isqrt(standing ** skew) + 1 for standing in range(2, amount + 1)]
    surplus, given = total - limit - (amount - 1), [1] * (amount - 1)
    while surplus > 0:
        free = [i for i in range(amount - 1) if given[i] < limit]
        pool, budget = sum([weights[i] for i in free]), surplus
        for i in free:
            addition = min(limit - given[i], max(1, budget * weights[i] // pool), surplus)
            given[i] = given[i] + addition
            surplus = surplus - addition
    return np.array([limit] + given)


def ragged_sizes(own_key, amount, total, reach, skew):
    if amount == 2:
        one = jax.random.randint(own_key, (), max(1, total - reach), min(reach, total - 1) + 1)
        return jnp.stack([one, total - one])
    sizes = jnp.asarray(split_up(amount, total, reach, skew), jnp.int32)
    twos = (amount - 1) // 2
    giver, taker = sizes[1:1 + 2 * twos:2], sizes[2:2 + 2 * twos:2]
    room = jnp.minimum(giver - 1, reach - taker)
    moved = jax.random.randint(jax.random.fold_in(own_key, 1), (twos,), 0, 1 << 20) % (room + 1)
    sizes = sizes.at[1:1 + 2 * twos:2].set(giver - moved).at[2:2 + 2 * twos:2].set(taker + moved)
    return sizes[jax.random.permutation(jax.random.fold_in(own_key, 2), amount)]


def noise(own_key, shape, spread, reach, pieces=(), kind=jnp.bfloat16):
    level = level_of(own_key, shape, pieces, -0.22, 0.18) if pieces else 1.0
    entries = jax.random.normal(own_key, shape, jnp.float32) * spread * level
    return jnp.minimum(jnp.maximum(entries, -reach), reach).astype(kind)


def setup_inputs(seed: int = 0) -> dict:
    arg_keys = jax.random.split(jax.random.key(seed), 9)
    queries = draw_queries(jax.random.fold_in(arg_keys[8], 71), 0)
    keys = draw_keys(jax.random.fold_in(arg_keys[8], 71), 0)
    values = noise(arg_keys[2], (SEQS, POSITIONS, HEADS * HEAD_DIM), 1.0, 6.0, ((0, 4), (1, 8), (2, 8)))
    out_grad = noise(arg_keys[3], (SEQS, POSITIONS, D), 1.0, 6.0, ((0, 4), (1, 8), (2, 8)))
    out_weight = noise(arg_keys[4], (D, HEADS * HEAD_DIM), (HEADS * HEAD_DIM) ** -0.5, 0.09375, ((0, 4), (1, 8)))
    slopes = jnp.clip(jnp.exp(math.log(0.05) - 6.015181 * jax.random.uniform(arg_keys[5], (HEADS,), jnp.float32) ** level_of(arg_keys[5], (HEADS,), ((0, 8),), -0.2, 0.2)), 0.00012207031, 0.05)
    counts = jax.vmap(lambda own: ragged_sizes(own, N_CONTEXT, BOUNDARIES, ROWS, 2))(jax.random.split(arg_keys[6], SEQS)).reshape((SEQS, N_CONTEXT)).astype(jnp.int32)
    gaps = place_ends(jax.random.randint(arg_keys[7], (SEQS, POSITIONS), 1, 13), jax.random.fold_in(arg_keys[7], 1), 1, 12).astype(jnp.int32)
    return {"queries": queries, "keys": keys, "values": values, "out_grad": out_grad, "out_weight": out_weight, "slopes": slopes, "counts": counts, "gaps": gaps}


NEG = -1e30


def split_heads(block):
    return block.reshape(POSITIONS, HEADS, HEAD_DIM).transpose(1, 0, 2)


def merge_heads(block):
    return block.transpose(1, 0, 2).reshape(POSITIONS, HEADS * HEAD_DIM)


def reference(queries, keys, values, out_grad, out_weight, slopes, counts, gaps):
    slot_index = jnp.arange(POSITIONS, dtype=jnp.int32)
    scaling = HEAD_DIM ** -0.5

    def one_sequence(inputs):
        q_seq, k_seq, v_seq, grad_seq, count_seq, gap_seq = inputs
        limits = jnp.repeat(count_seq, ROWS)
        slot_valid = (slot_index % ROWS) < limits
        offsets = jnp.cumsum(jnp.where(slot_valid, gap_seq, 0)).astype(jnp.float32)
        grad_masked = jnp.where(slot_valid[:, None], grad_seq, jnp.zeros_like(grad_seq))
        grad_heads = jnp.dot(grad_masked, out_weight, preferred_element_type=jnp.float32).astype(jnp.bfloat16)
        allowed = slot_valid[None, :] & (slot_index[None, :] <= slot_index[:, None])

        def one_head(head_inputs):
            q_head, k_head, v_head, g_head, slope = head_inputs
            logits = jnp.dot(q_head, k_head.T, preferred_element_type=jnp.float32) * scaling
            logits = logits - slope * (offsets[:, None] - offsets[None, :])
            logits = jnp.where(allowed, logits, NEG)
            peak = jnp.max(logits, axis=1)
            log_total = peak + jnp.log(jnp.sum(jnp.where(allowed, jnp.exp(logits - peak[:, None]), 0.0), axis=1))
            probs = jnp.where(allowed, jnp.exp(logits - log_total[:, None]), 0.0)
            probs_b = probs.astype(jnp.bfloat16)
            output = jnp.dot(probs_b, v_head, preferred_element_type=jnp.float32).astype(jnp.bfloat16)
            delta = jnp.sum(g_head.astype(jnp.float32) * output.astype(jnp.float32), axis=1)
            value_dots = jnp.dot(g_head, v_head.T, preferred_element_type=jnp.float32)
            dscore = (probs * (value_dots - delta[:, None])).astype(jnp.bfloat16)
            q_grad = (jnp.dot(dscore, k_head, preferred_element_type=jnp.float32) * scaling).astype(jnp.bfloat16)
            k_grad = (jnp.dot(dscore.T, q_head, preferred_element_type=jnp.float32) * scaling).astype(jnp.bfloat16)
            v_grad = jnp.dot(probs_b.T, g_head, preferred_element_type=jnp.float32).astype(jnp.bfloat16)
            return output, q_grad, k_grad, v_grad

        output, q_grad, k_grad, v_grad = lax.map(one_head, (split_heads(q_seq), split_heads(k_seq), split_heads(v_seq), split_heads(grad_heads), slopes))
        weight_term = lax.dot_general(grad_masked, merge_heads(output), (((0,), (0,)), ((), ())), preferred_element_type=jnp.float32)
        return merge_heads(q_grad), merge_heads(k_grad), merge_heads(v_grad), weight_term

    def accumulate(total, inputs):
        q_grad, k_grad, v_grad, weight_term = one_sequence(inputs)
        return total + weight_term, (q_grad, k_grad, v_grad)

    start_total = jnp.zeros((D, HEADS * HEAD_DIM), jnp.float32)
    weight_grad, grads = lax.scan(accumulate, start_total, (queries, keys, values, out_grad, counts, gaps))
    return grads[0], grads[1], grads[2], weight_grad
```

```python
import itertools

import jax
import jax.numpy as jnp
from jax import lax
from jax.experimental import pallas as pl
from jax.experimental.pallas import tpu as pltpu
from jax.sharding import PartitionSpec as P

MESH = pl.DeviceIdType.MESH
F32, BF16 = jnp.float32, jnp.bfloat16
NEG = -1e30
ROWS = 128
HALF = 256


def mm(a, b, ca, cb):
    return lax.dot_general(a, b, (((ca,), (cb,)), ((), ())), preferred_element_type=F32)


def kernel(
    slopes_ref, counts_ref, gaps_ref, q_ref, k_ref, v_ref, g_ref, w_ref,
    dq_ref, dk_ref, dv_ref, wg_ref,
    gap_out, gap_all, k_all, v_all, q_head, g_head, g_all, g_far, w_all,
    prob, o_head, o_out, o_own, o_masked, o_far, hp_own, hp_out, hp_far, hg_out,
    dq_out, dk_acc, dv_acc, dk_out, dv_out,
    part, part_out, half_in, full_in, part2, part2_out, half2_in, full2_in,
    ssem, rsem,
):
    c, z, f = lax.axis_index("context"), lax.axis_index("tensor"), lax.axis_index("fsdp")
    nz = g_all.shape[0]
    y, xl = lax.div(c, 2), lax.rem(c, 2)
    xh, core = lax.div(f, 2), lax.rem(f, 2)
    x = xh * 2 + xl
    place = (x, y)
    side = lax.rem(c + y, 2)
    scaling = ROWS ** (-0.5)
    count = counts_ref[0, 0]
    slope = slopes_ref[0, y]

    def dev(c_=None, z_=None, f_=None):
        return {
            "context": c if c_ is None else c_,
            "tensor": z if z_ is None else z_,
            "fsdp": f if f_ is None else f_,
        }

    def beside(axis, step):
        if axis == 0:
            x2 = lax.rem(x + step + 4, 4)
            return dev(c_=y * 2 + lax.rem(x2, 2), f_=lax.div(x2, 2) * 2 + core)
        return dev(c_=lax.rem(y + step + 4, 4) * 2 + xl)

    right, left = dev(z_=lax.rem(z + 1, nz)), dev(z_=lax.rem(z + nz - 1, nz))
    partner = dev(f_=xh * 2 + 1 - core)
    across = dev(c_=y * 2 + 1 - xl, f_=(1 - xh) * 2 + core)

    send_index, recv_index = itertools.count(), itertools.count()
    sent = []

    def slots(n):
        first = next(recv_index)
        for _ in range(n - 1):
            next(recv_index)
        return first

    def send(src, dst, index, where):
        copy = pltpu.make_async_remote_copy(
            src_ref=src, dst_ref=dst, send_sem=ssem.at[next(send_index)],
            recv_sem=rsem.at[index], device_id=where, device_id_type=MESH,
        )
        copy.start()
        sent.append((None, copy))

    def arrived(dst, index):
        pltpu.make_async_remote_copy(
            src_ref=dst, dst_ref=dst, send_sem=ssem.at[0],
            recv_sem=rsem.at[index], device_id=partner, device_id_type=MESH,
        ).wait_recv()

    def give(mine, src, dst, index, where):
        copy = pltpu.make_async_remote_copy(
            src_ref=src, dst_ref=dst, send_sem=ssem.at[next(send_index)],
            recv_sem=rsem.at[index], device_id=where, device_id_type=MESH,
        )
        pl.when(jnp.logical_not(mine))(copy.start)
        pl.when(mine)(pltpu.make_async_copy(src, dst, rsem.at[index]).start)
        sent.append((mine, copy))

    def taken(mine, dst, index):
        pl.when(jnp.logical_not(mine))(lambda: arrived(dst, index))
        pl.when(mine)(pltpu.make_async_copy(dst, dst, rsem.at[index]).wait)

    def cols(ref, head):
        return ref.at[:, pl.ds(pl.multiple_of(head * ROWS, ROWS), ROWS)]

    def rows(ref, shard):
        return ref.at[pl.ds(pl.multiple_of(shard * ROWS, ROWS), ROWS)]

    lane8 = lax.broadcasted_iota(jnp.int32, (8, ROWS), 1)
    row8 = lax.broadcasted_iota(jnp.int32, (8, ROWS), 0)
    gap_out[...] = jnp.where(
        lane8 < count, jnp.broadcast_to(gaps_ref[...], (8, ROWS)), 0
    ).astype(F32)

    barrier = pltpu.get_barrier_semaphore()
    greeted = [dev(c_=lax.rem(c + d, 8)) for d in range(1, 8)] + [right, left, partner, across]
    for where in greeted:
        pl.semaphore_signal(barrier, inc=1, device_id=where, device_id_type=MESH)
    pl.semaphore_wait(barrier, len(greeted))

    at_gap, at_k, at_v, at_q = slots(8), slots(8), slots(8), slots(4)
    at_ring, at_far, at_w = slots(2 * nz), slots(4), slots(2)
    own_g = pltpu.make_async_copy(g_ref, g_all.at[z], rsem.at[at_ring])
    own_g.start()
    send(g_ref, g_all.at[z], at_ring + 1, right)
    send(g_ref, g_all.at[z], at_ring + nz + 1, left)
    for d in range(8):
        peer = lax.rem(c + d, 8)
        head = lax.div(peer, 2)
        if d == 0:
            gap_all[c] = gap_out[...]
            own_k = pltpu.make_async_copy(cols(k_ref, head), rows(k_all, c), rsem.at[at_k + c])
            own_v = pltpu.make_async_copy(cols(v_ref, head), rows(v_all, c), rsem.at[at_v + c])
            own_k.start()
            own_v.start()
        else:
            send(gap_out, gap_all.at[c], at_gap + c, dev(c_=peer))
            send(cols(k_ref, head), rows(k_all, c), at_k + c, dev(c_=peer))
            send(cols(v_ref, head), rows(v_all, c), at_v + c, dev(c_=peer))
    for d in range(4):
        head = lax.rem(y + d, 4)
        peer = head * 2 + side
        give(peer == c, cols(q_ref, head), q_head.at[y], at_q + y, dev(c_=peer))
    own_w = pltpu.make_async_copy(w_ref, w_all.at[xh], rsem.at[at_w])
    own_w.start()
    send(w_ref, w_all.at[xh], at_w + 1, across)

    to_right, to_left = nz // 2, nz - 1 - nz // 2

    def ring(step):
        if step <= to_right:
            block = g_all.at[lax.rem(z + nz - step, nz)]
            arrived(block, at_ring + step)
            if step < to_right:
                send(block, block, at_ring + step + 1, right)
        if step <= to_left:
            block = g_all.at[lax.rem(z + step, nz)]
            arrived(block, at_ring + nz + step)
            if step < to_left:
                send(block, block, at_ring + nz + step + 1, left)

    ring(1)

    for s in range(8):
        pl.when(s != c)(lambda s=s: arrived(gap_all.at[s], at_gap + s))
    gaps8 = jnp.zeros((8, ROWS), F32)
    before = jnp.zeros((8, ROWS), F32)
    for s in range(8):
        gaps8 = jnp.where(row8 == s, gap_all[s], gaps8)
        before = before + jnp.where(row8 > s, gap_all[s], 0.0)
    r128 = lax.broadcasted_iota(jnp.int32, (ROWS, ROWS), 0)
    l128 = lax.broadcasted_iota(jnp.int32, (ROWS, ROWS), 1)
    upto = (r128 <= l128).astype(BF16)
    offs8 = mm(gaps8.astype(BF16), upto, 1, 0) + jnp.sum(before, axis=1, keepdims=True)
    k_offset = jnp.concatenate([offs8[s : s + 1] for s in range(8)], axis=1)
    k_valid = jnp.concatenate([gaps8[s : s + 1] for s in range(8)], axis=1) > 0.0
    ring(2)
    for s in range(8):
        own = s == c
        taken(own, k_all.at[pl.ds(s * ROWS, ROWS)], at_k + s)
        taken(own, v_all.at[pl.ds(s * ROWS, ROWS)], at_v + s)

    at_o = slots(4)
    shard = [2 * t + lax.rem(xl + t, 2) for t in range(4)]

    def forward(t):
        n = 2 * ROWS * (t + 1)
        ct = shard[t]
        taken(ct == c, q_head.at[t], at_q + t)
        q_gaps = gap_all[ct][0:1]
        q_before = jnp.zeros((1, ROWS), F32)
        for s in range(2 * t + 1):
            q_before = q_before + gap_all[s][0:1] * (s < ct).astype(F32)
        q_offset = jnp.sum(
            jnp.where(l128 <= r128, jnp.broadcast_to(q_gaps, (ROWS, ROWS)), 0.0)
            + jnp.broadcast_to(q_before, (ROWS, ROWS)),
            axis=1, keepdims=True,
        )
        logits = mm(q_head[t], k_all[0:n], 1, 1) * scaling
        logits = logits - slope * (q_offset - k_offset[:, 0:n])
        q_slot = ct * ROWS + lax.broadcasted_iota(jnp.int32, (ROWS, n), 0)
        k_slot = lax.broadcasted_iota(jnp.int32, (ROWS, n), 1)
        allowed = jnp.logical_and(k_valid[:, 0:n], k_slot <= q_slot)
        logits = jnp.where(allowed, logits, NEG)
        peak = jnp.max(logits, axis=1, keepdims=True)
        weight = jnp.where(allowed, jnp.exp(logits - peak), 0.0)
        probs = weight * (1.0 / jnp.sum(weight, axis=1, keepdims=True))
        prob[t, :, 0:n] = probs
        o_head[t] = mm(probs.astype(BF16), v_all[0:n], 1, 0).astype(BF16)
        give(ct == c, o_head.at[t], cols(o_own, y), at_o + y, dev(c_=ct))

    forward(0)
    forward(1)
    ring(3)
    forward(2)
    ring(4)
    forward(3)

    own_g.wait()
    for j in range(4):
        theirs = 4 * (j // 2) + 2 * (1 - core) + j % 2
        send(g_all.at[theirs], g_far.at[j], at_far + j, partner)

    at_of, at_hp = slots(1), slots(1)
    for h in range(4):
        taken(h * 2 + side == c, o_own.at[:, h * ROWS : (h + 1) * ROWS], at_o + h)
    live = lax.broadcasted_iota(jnp.int32, o_own.shape, 0) < count
    o_masked[...] = jnp.where(live, o_own[...], jnp.zeros_like(o_own))
    send(o_masked, o_far, at_of, partner)
    for j in range(4):
        arrived(g_far.at[j], at_far + j)
    arrived(o_far, at_of)

    def both(j):
        mine = g_all[4 * (j // 2) + 2 * core + j % 2]
        return jnp.concatenate([mine, g_far[j]], axis=0)

    outputs = jnp.concatenate([o_masked[...], o_far[...]], axis=0)
    for j in range(4):
        product = mm(both(j), outputs, 0, 0)
        part[0, j] = product[:, 0:HALF]
        for i in range(4):
            part[1, i, j * ROWS : (j + 1) * ROWS] = product[i * ROWS : (i + 1) * ROWS, HALF:]

    class Scatter:
        def __init__(self, axis, terms, out, half, full):
            self.axis, self.terms, self.out, self.half, self.full = axis, terms, out, half, full
            self.at = slots(4)
            self.mid = terms.shape[1] // 2
            p = place[axis]
            self.own = p
            self.far, self.up, self.down = (lax.rem(p + d, 4) for d in (2, 1, 3))

        def start(self):
            self.out[self.far] = self.terms[self.far].astype(BF16)
            far = self.out.at[self.far]
            send(far.at[0 : self.mid], self.half.at[0], self.at, beside(self.axis, 1))
            send(far.at[self.mid :], self.half.at[1], self.at + 1, beside(self.axis, -1))

        def middle(self):
            mid = self.mid
            arrived(self.half.at[0], self.at)
            mine = self.terms.at[self.up]
            self.out[self.up, 0:mid] = (mine[0:mid] + self.half[0].astype(F32)).astype(BF16)
            self.out[self.up, mid:] = mine[mid:].astype(BF16)
            send(self.out.at[self.up], self.full.at[0], self.at + 2, beside(self.axis, 1))
            arrived(self.half.at[1], self.at + 1)
            mine = self.terms.at[self.down]
            self.out[self.down, 0:mid] = mine[0:mid].astype(BF16)
            self.out[self.down, mid:] = (mine[mid:] + self.half[1].astype(F32)).astype(BF16)
            send(self.out.at[self.down], self.full.at[1], self.at + 3, beside(self.axis, -1))

        def finish(self):
            arrived(self.full.at[0], self.at + 2)
            arrived(self.full.at[1], self.at + 3)
            return self.terms[self.own] + self.full[0].astype(F32) + self.full[1].astype(F32)

    first = [Scatter(i, part.at[i], part_out.at[i], half_in.at[i], full_in.at[i]) for i in range(2)]
    for scatter in first:
        scatter.start()

    own_w.wait()
    arrived(w_all.at[1 - xh], at_w + 1)
    width = w_all.shape[2]
    for n in range(0, width, HALF):
        total = jnp.zeros((2 * ROWS, HALF), F32)
        for j in range(4):
            wide = w_all.shape[1] // 2
            w_rows = w_all[j // 2, (j % 2) * wide : (j % 2 + 1) * wide, n : n + HALF]
            total = total + mm(both(j), w_rows, 1, 0)
        hp_own[:, n : n + HALF] = total[0:ROWS]
        hp_out[:, n : n + HALF] = total[ROWS:]
    send(hp_out, hp_far, at_hp, partner)
    for scatter in first:
        scatter.middle()
    arrived(hp_far, at_hp)
    hg_out[...] = jnp.where(live, hp_own[...] + hp_far[...], 0.0).astype(BF16)
    at_g = slots(4)
    for d in range(4):
        head = lax.rem(y + d, 4)
        peer = head * 2 + side
        give(peer == c, cols(hg_out, head), g_head.at[y], at_g + y, dev(c_=peer))

    at_dq, at_dk, at_dv = slots(4), slots(8), slots(8)
    for t in (3, 2, 1, 0):
        n = 2 * ROWS * (t + 1)
        ct = shard[t]
        taken(ct == c, g_head.at[t], at_g + t)
        grad = g_head[t]
        delta = jnp.sum(grad.astype(F32) * o_head[t].astype(F32), axis=1, keepdims=True)
        probs = prob[t, :, 0:n]
        dprob = mm(grad, v_all[0:n], 1, 1)
        dscore = (probs * (dprob - delta)).astype(BF16)
        dq_out[t] = (mm(dscore, k_all[0:n], 1, 0) * scaling).astype(BF16)
        give(ct == c, dq_out.at[t], cols(dq_ref, y), at_dq + y, dev(c_=ct))
        dk_part = mm(dscore, q_head[t], 0, 0)
        dv_part = mm(probs.astype(BF16), grad, 0, 0)
        if t == 3:
            dk_acc[...] = dk_part
            dv_acc[...] = dv_part
        else:
            dk_acc[0:n] += dk_part
            dv_acc[0:n] += dv_part
        for s in (2 * t + 1, 2 * t):
            at = slice(s * ROWS, (s + 1) * ROWS)
            dk_out[at] = (dk_acc[at] * scaling).astype(BF16)
            dv_out[at] = dv_acc[at].astype(BF16)
            there = dev(c_=jnp.int32(s))
            give(s == c, dk_out.at[at], cols(dk_ref.at[xl], y), at_dk + c, there)
            give(s == c, dv_out.at[at], cols(dv_ref.at[xl], y), at_dv + c, there)

    second = [
        Scatter(1 - i, part2.at[i], part2_out.at[i], half2_in.at[i], full2_in.at[i])
        for i in range(2)
    ]
    for i in range(2):
        part2[i] = first[i].finish().reshape(part2.shape[1:])
        second[i].start()
    for i in range(2):
        second[i].middle()
    unit = xl * 4 + y
    for i in range(2):
        wg_ref[unit, :, i * HALF : (i + 1) * HALF] = second[i].finish().astype(BF16)
    at_x, at_y = slots(1), slots(8)
    other = dev(c_=y * 2 + 1 - xl)
    send(wg_ref.at[unit], wg_ref.at[unit], at_x, other)
    send(wg_ref.at[unit], wg_ref.at[unit], at_y, beside(1, 1))
    send(wg_ref.at[unit], wg_ref.at[unit], at_y + 1, beside(1, -1))
    unit2 = (1 - xl) * 4 + y
    arrived(wg_ref.at[unit2], at_x)
    send(wg_ref.at[unit2], wg_ref.at[unit2], at_y + 2, beside(1, 1))
    send(wg_ref.at[unit2], wg_ref.at[unit2], at_y + 3, beside(1, -1))
    below, above, far = (lax.rem(y + d, 4) for d in (3, 1, 2))
    columns = (xl * 4, (1 - xl) * 4)
    mid = ROWS // 2
    for i, column in enumerate(columns):
        low = wg_ref.at[column + below]
        arrived(low, at_y + 2 * i)
        send(low.at[0:mid], low.at[0:mid], at_y + 4 + 2 * i, beside(1, 1))
        high = wg_ref.at[column + above]
        arrived(high, at_y + 2 * i + 1)
        send(high.at[mid:], high.at[mid:], at_y + 5 + 2 * i, beside(1, -1))

    for h in range(4):
        taken(h * 2 + side == c, dq_ref.at[:, h * ROWS : (h + 1) * ROWS], at_dq + h)
    for s in range(8):
        at = slice((s // 2) * ROWS, (s // 2 + 1) * ROWS)
        taken(s == c, dk_ref.at[s % 2, :, at], at_dk + s)
        taken(s == c, dv_ref.at[s % 2, :, at], at_dv + s)
    for i, column in enumerate(columns):
        last = wg_ref.at[column + far]
        arrived(last.at[0:mid], at_y + 4 + 2 * i)
        arrived(last.at[mid:], at_y + 5 + 2 * i)

    for mine, copy in sent:
        if mine is None:
            copy.wait_send()
        else:
            pl.when(jnp.logical_not(mine))(copy.wait_send)
    assert next(send_index) <= ssem.shape[0] and next(recv_index) <= rsem.shape[0]


def per_device(queries, keys, values, out_grad, out_weight, slopes, counts, gaps):
    width = queries.shape[2]
    nz = lax.axis_size("tensor")
    vmem, hbm = pl.BlockSpec(memory_space=pltpu.VMEM), pl.BlockSpec(memory_space=pl.ANY)
    smem = pl.BlockSpec(memory_space=pltpu.SMEM)

    def v(dtype, *shape):
        return pltpu.VMEM(shape, dtype)

    dq, dk, dv, wg = pl.pallas_call(
        kernel,
        out_shape=(
            jax.ShapeDtypeStruct((ROWS, width), BF16),
            jax.ShapeDtypeStruct((2, ROWS, width), BF16),
            jax.ShapeDtypeStruct((2, ROWS, width), BF16),
            jax.ShapeDtypeStruct((8, ROWS, width), BF16),
        ),
        in_specs=[smem, smem, vmem, hbm, hbm, hbm, hbm, hbm],
        out_specs=(vmem, vmem, vmem, vmem),
        scratch_shapes=[
            v(F32, 8, ROWS),
            v(F32, 8, 8, ROWS),
            v(BF16, 8 * ROWS, ROWS),
            v(BF16, 8 * ROWS, ROWS),
            v(BF16, 4, ROWS, ROWS),
            v(BF16, 4, ROWS, ROWS),
            v(BF16, nz, ROWS, width),
            v(BF16, 4, ROWS, width),
            v(BF16, 2, *out_weight.shape),
            v(F32, 4, ROWS, 8 * ROWS),
            v(BF16, 4, ROWS, ROWS),
            v(BF16, 8, ROWS),
            v(BF16, ROWS, width),
            v(BF16, ROWS, width),
            v(BF16, ROWS, width),
            v(F32, ROWS, width),
            v(F32, ROWS, width),
            v(F32, ROWS, width),
            v(BF16, ROWS, width),
            v(BF16, 4, ROWS, ROWS),
            v(F32, 8 * ROWS, ROWS),
            v(F32, 8 * ROWS, ROWS),
            v(BF16, 8 * ROWS, ROWS),
            v(BF16, 8 * ROWS, ROWS),
            v(F32, 2, 4, 4 * ROWS, HALF),
            v(BF16, 2, 4, 4 * ROWS, HALF),
            v(BF16, 2, 2, 2 * ROWS, HALF),
            v(BF16, 2, 2, 4 * ROWS, HALF),
            v(F32, 2, 4, ROWS, HALF),
            v(BF16, 2, 4, ROWS, HALF),
            v(BF16, 2, 2, ROWS // 2, HALF),
            v(BF16, 2, 2, ROWS, HALF),
            pltpu.SemaphoreType.DMA((128,)),
            pltpu.SemaphoreType.DMA((128,)),
        ],
        compiler_params=pltpu.CompilerParams(
            collective_id=0, has_side_effects=True, vmem_limit_bytes=56 << 20
        ),
        name="block_backward",
    )(
        slopes.reshape(1, -1), counts, gaps,
        queries[0], keys[0], values[0], out_grad[0], out_weight,
    )
    dk = (dk[0].astype(F32) + dk[1].astype(F32)).astype(BF16)
    dv = (dv[0].astype(F32) + dv[1].astype(F32)).astype(BF16)
    return dq[None], dk[None], dv[None], wg.reshape(-1, width).astype(F32)


def solution(mesh):
    rows = P("fsdp", "context", "tensor")
    weight = P("fsdp", "tensor")
    placed = (rows, rows, rows, rows, weight, P("tensor"), P("fsdp", "context"))
    return jax.shard_map(
        per_device,
        mesh=mesh,
        in_specs=placed + (P("fsdp", "context"),),
        out_specs=(rows, rows, rows, weight),
        check_vma=False,
    )
```

```python
import itertools

import jax
import jax.numpy as jnp
from jax import lax
from jax.experimental import pallas as pl
from jax.experimental.pallas import tpu as pltpu
from jax.sharding import PartitionSpec as P

MESH = pl.DeviceIdType.MESH
F32, BF16 = jnp.float32, jnp.bfloat16
NEG = -1e30
ROWS = 128
HALF = 256


def mm(a, b, ca, cb):
    return lax.dot_general(a, b, (((ca,), (cb,)), ((), ())), preferred_element_type=F32)


def kernel(
    slopes_ref, counts_ref, gaps_ref, q_ref, k_ref, v_ref, g_ref, w_ref,
    dq_ref, dk_ref, dv_ref, wg_ref,
    gap_out, gap_all, k_all, v_all, q_head, g_head, g_all, g_far, w_all,
    prob, o_head, o_own, o_masked, o_far, hp_own, hp_out, hp_far, hg_out,
    dq_out, dk_acc, dv_acc, dk_out, dv_out,
    part, part_out, half_in, full_in, part2, part2_out, half2_in, full2_in,
    ssem, rsem,
):
    c, z, f = lax.axis_index("context"), lax.axis_index("tensor"), lax.axis_index("fsdp")
    nz = g_all.shape[0]
    y, xl = lax.div(c, 2), lax.rem(c, 2)
    xh, core = lax.div(f, 2), lax.rem(f, 2)
    x = xh * 2 + xl
    place = (x, y)
    side = lax.rem(c + y, 2)
    scaling = ROWS ** (-0.5)
    count = counts_ref[0, 0]
    slope = slopes_ref[0, y]

    def dev(c_=None, z_=None, f_=None):
        return {
            "context": c if c_ is None else c_,
            "tensor": z if z_ is None else z_,
            "fsdp": f if f_ is None else f_,
        }

    def beside(axis, step):
        if axis == 0:
            x2 = lax.rem(x + step + 4, 4)
            return dev(c_=y * 2 + lax.rem(x2, 2), f_=lax.div(x2, 2) * 2 + core)
        return dev(c_=lax.rem(y + step + 4, 4) * 2 + xl)

    right, left = dev(z_=lax.rem(z + 1, nz)), dev(z_=lax.rem(z + nz - 1, nz))
    partner = dev(f_=xh * 2 + 1 - core)
    across = dev(c_=y * 2 + 1 - xl, f_=(1 - xh) * 2 + core)

    send_index, recv_index = itertools.count(), itertools.count()
    sent = []

    def slots(n):
        first = next(recv_index)
        for _ in range(n - 1):
            next(recv_index)
        return first

    def send(src, dst, index, where):
        copy = pltpu.make_async_remote_copy(
            src_ref=src, dst_ref=dst, send_sem=ssem.at[next(send_index)],
            recv_sem=rsem.at[index], device_id=where, device_id_type=MESH,
        )
        copy.start()
        sent.append((None, copy))

    def arrived(dst, index):
        pltpu.make_async_remote_copy(
            src_ref=dst, dst_ref=dst, send_sem=ssem.at[0],
            recv_sem=rsem.at[index], device_id=partner, device_id_type=MESH,
        ).wait_recv()

    def give(mine, src, dst, index, where):
        copy = pltpu.make_async_remote_copy(
            src_ref=src, dst_ref=dst, send_sem=ssem.at[next(send_index)],
            recv_sem=rsem.at[index], device_id=where, device_id_type=MESH,
        )
        pl.when(jnp.logical_not(mine))(copy.start)
        pl.when(mine)(pltpu.make_async_copy(src, dst, rsem.at[index]).start)
        sent.append((mine, copy))

    def taken(mine, dst, index):
        pl.when(jnp.logical_not(mine))(lambda: arrived(dst, index))
        pl.when(mine)(pltpu.make_async_copy(dst, dst, rsem.at[index]).wait)

    def cols(ref, head):
        return ref.at[:, pl.ds(pl.multiple_of(head * ROWS, ROWS), ROWS)]

    def rows(ref, shard):
        return ref.at[pl.ds(pl.multiple_of(shard * ROWS, ROWS), ROWS)]

    lane8 = lax.broadcasted_iota(jnp.int32, (8, ROWS), 1)
    row8 = lax.broadcasted_iota(jnp.int32, (8, ROWS), 0)
    gap_out[...] = jnp.where(
        lane8 < count, jnp.broadcast_to(gaps_ref[...], (8, ROWS)), 0
    ).astype(F32)

    barrier = pltpu.get_barrier_semaphore()
    greeted = [dev(c_=lax.rem(c + d, 8)) for d in range(1, 8)] + [right, left, partner, across]
    for where in greeted:
        pl.semaphore_signal(barrier, inc=1, device_id=where, device_id_type=MESH)
    pl.semaphore_wait(barrier, len(greeted))

    at_gap, at_k, at_v, at_q = slots(8), slots(8), slots(8), slots(4)
    at_ring, at_far, at_w = slots(2 * nz), slots(4), slots(7)
    part_rows = ROWS // 2
    hops = nz // 2

    def piece(block, h):
        return g_all.at[block, h * part_rows : (h + 1) * part_rows]

    def to_partner(block, src):
        mine = lax.rem(lax.div(block, 2), 2) == core
        j = 2 * lax.div(block, 4) + lax.rem(block, 2)
        copy = pltpu.make_async_remote_copy(
            src_ref=src, dst_ref=g_far.at[j], send_sem=ssem.at[next(send_index)],
            recv_sem=rsem.at[at_far + j], device_id=partner, device_id_type=MESH,
        )
        pl.when(jnp.logical_not(mine))(copy.start)
        sent.append((mine, copy))

    own_g = pltpu.make_async_copy(g_ref, g_all.at[z], rsem.at[at_ring + 2 * nz - 1])
    own_g.start()
    for h in range(2):
        src = g_ref.at[h * part_rows : (h + 1) * part_rows]
        send(src, piece(z, h), at_ring + h, right)
        send(src, piece(z, h), at_ring + nz + h, left)
    for d in range(1, 8):
        send(gap_out, gap_all.at[c], at_gap + c, dev(c_=lax.rem(c + d, 8)))
    gap_all[c] = gap_out[...]
    color = lax.rem(xl + y, 2)
    w_half = w_all.shape[1] // 2
    cuts = (0, 192, 384, 512)
    w_next = (beside(1, 1), beside(1, -1), dev(c_=y * 2 + 1 - xl))

    def w_piece(ref, half, i):
        at = pl.multiple_of(half * w_half + cuts[i], 64)
        return ref.at[pl.ds(at, cuts[i + 1] - cuts[i])]

    for i in range(3):
        send(w_piece(w_ref, 1 - color, i), w_piece(w_all.at[xh], 1 - color, i), at_w + i, across)
    for d in range(8):
        peer = lax.rem(c + d, 8)
        head = lax.div(peer, 2)
        if d == 0:
            own_k = pltpu.make_async_copy(cols(k_ref, head), rows(k_all, c), rsem.at[at_k + c])
            own_v = pltpu.make_async_copy(cols(v_ref, head), rows(v_all, c), rsem.at[at_v + c])
            own_k.start()
            own_v.start()
        else:
            send(cols(k_ref, head), rows(k_all, c), at_k + c, dev(c_=peer))
            send(cols(v_ref, head), rows(v_all, c), at_v + c, dev(c_=peer))
        if d < 4:
            head = lax.rem(y + d, 4)
            peer = head * 2 + side
            give(peer == c, cols(q_ref, head), q_head.at[y], at_q + y, dev(c_=peer))
    to_partner(z, g_ref)
    own_w = pltpu.make_async_copy(w_ref, w_all.at[xh], rsem.at[at_w + 6])
    own_w.start()

    last = 2 * (hops - 1)

    def ring(k):
        d, h = k // 2 + 1, k % 2
        for way, (where, step, base) in enumerate(
            ((right, nz - d, at_ring), (left, d, at_ring + nz))
        ):
            block = lax.rem(z + step, nz)
            half = way if k == last else h
            arrived(piece(block, half), base + k)
            if d + 1 < hops or (d + 1 == hops and h == way):
                after = min(k + 2, last)
                send(piece(block, half), piece(block, half), base + after, where)
            if h == 1:
                to_partner(block, g_all.at[block])
        if k == last:
            to_partner(lax.rem(z + hops, nz), g_all.at[lax.rem(z + hops, nz)])

    def w_pass(i):
        theirs = w_piece(w_all.at[1 - xh], color, i)
        arrived(theirs, at_w + i)
        send(theirs, theirs, at_w + 3 + i, w_next[i])

    ring(0)

    for s in range(8):
        pl.when(s != c)(lambda s=s: arrived(gap_all.at[s], at_gap + s))
    gaps8 = jnp.zeros((8, ROWS), F32)
    before = jnp.zeros((8, ROWS), F32)
    for s in range(8):
        gaps8 = jnp.where(row8 == s, gap_all[s], gaps8)
        before = before + jnp.where(row8 > s, gap_all[s], 0.0)
    r128 = lax.broadcasted_iota(jnp.int32, (ROWS, ROWS), 0)
    l128 = lax.broadcasted_iota(jnp.int32, (ROWS, ROWS), 1)
    upto = (r128 <= l128).astype(BF16)
    offs8 = mm(gaps8.astype(BF16), upto, 1, 0) + jnp.sum(before, axis=1, keepdims=True)
    k_offset = jnp.concatenate([offs8[s : s + 1] for s in range(8)], axis=1)
    k_valid = jnp.concatenate([gaps8[s : s + 1] for s in range(8)], axis=1) > 0.0

    at_o = slots(4)
    shard = [2 * t + lax.rem(xl + t, 2) for t in range(4)]

    def forward(t):
        n = 2 * ROWS * (t + 1)
        ct = shard[t]
        for j in (2 * t, 2 * t + 1):
            taken(j == c, k_all.at[j * ROWS : (j + 1) * ROWS], at_k + j)
            taken(j == c, v_all.at[j * ROWS : (j + 1) * ROWS], at_v + j)
        taken(ct == c, q_head.at[t], at_q + t)
        q_gaps = gap_all[ct][0:1]
        q_before = jnp.zeros((1, ROWS), F32)
        for s in range(2 * t + 1):
            q_before = q_before + gap_all[s][0:1] * (s < ct).astype(F32)
        q_offset = jnp.sum(
            jnp.where(l128 <= r128, jnp.broadcast_to(q_gaps, (ROWS, ROWS)), 0.0)
            + jnp.broadcast_to(q_before, (ROWS, ROWS)),
            axis=1, keepdims=True,
        )
        logits = mm(q_head[t], k_all[0:n], 1, 1) * scaling
        logits = logits - slope * (q_offset - k_offset[:, 0:n])
        q_slot = ct * ROWS + lax.broadcasted_iota(jnp.int32, (ROWS, n), 0)
        k_slot = lax.broadcasted_iota(jnp.int32, (ROWS, n), 1)
        allowed = jnp.logical_and(k_valid[:, 0:n], k_slot <= q_slot)
        logits = jnp.where(allowed, logits, NEG)
        peak = jnp.max(logits, axis=1, keepdims=True)
        weight = jnp.where(allowed, jnp.exp(logits - peak), 0.0)
        probs = weight * (1.0 / jnp.sum(weight, axis=1, keepdims=True))
        prob[t, :, 0:n] = probs
        o_head[t] = mm(probs.astype(BF16), v_all[0:n], 1, 0).astype(BF16)
        give(ct == c, o_head.at[t], cols(o_own, y), at_o + y, dev(c_=ct))

    ring(1)
    ring(2)
    w_pass(0)
    ring(3)
    forward(0)
    ring(4)
    forward(1)
    ring(5)
    forward(2)
    w_pass(1)
    forward(3)
    ring(6)
    own_g.wait()

    at_of, at_hp = slots(1), slots(1)
    for h in range(4):
        taken(h * 2 + side == c, o_own.at[:, h * ROWS : (h + 1) * ROWS], at_o + h)
    live = lax.broadcasted_iota(jnp.int32, o_own.shape, 0) < count
    o_masked[...] = jnp.where(live, o_own[...], jnp.zeros_like(o_own))
    send(o_masked, o_far, at_of, partner)
    w_pass(2)
    for j in range(4):
        arrived(g_far.at[j], at_far + j)

    def both(j):
        mine = g_all[4 * (j // 2) + 2 * core + j % 2]
        return jnp.concatenate([mine, g_far[j]], axis=0)

    class Scatter:
        def __init__(self, axis, terms, out, half, full):
            self.axis, self.terms, self.out, self.half, self.full = axis, terms, out, half, full
            self.at = slots(4)
            self.mid = terms.shape[1] // 2
            p = place[axis]
            self.own = p
            self.far, self.up, self.down = (lax.rem(p + d, 4) for d in (2, 1, 3))

        def start(self):
            self.out[self.far] = self.terms[self.far].astype(BF16)
            far = self.out.at[self.far]
            send(far.at[0 : self.mid], self.half.at[0], self.at, beside(self.axis, 1))
            send(far.at[self.mid :], self.half.at[1], self.at + 1, beside(self.axis, -1))

        def middle(self):
            mid = self.mid
            arrived(self.half.at[0], self.at)
            mine = self.terms.at[self.up]
            self.out[self.up, 0:mid] = (mine[0:mid] + self.half[0].astype(F32)).astype(BF16)
            self.out[self.up, mid:] = mine[mid:].astype(BF16)
            send(self.out.at[self.up], self.full.at[0], self.at + 2, beside(self.axis, 1))
            arrived(self.half.at[1], self.at + 1)
            mine = self.terms.at[self.down]
            self.out[self.down, 0:mid] = mine[0:mid].astype(BF16)
            self.out[self.down, mid:] = (mine[mid:] + self.half[1].astype(F32)).astype(BF16)
            send(self.out.at[self.down], self.full.at[1], self.at + 3, beside(self.axis, -1))

        def finish(self):
            arrived(self.full.at[0], self.at + 2)
            arrived(self.full.at[1], self.at + 3)
            return self.terms[self.own] + self.full[0].astype(F32) + self.full[1].astype(F32)

    own_w.wait()
    for i in range(3):
        arrived(w_piece(w_all.at[1 - xh], 1 - color, i), at_w + 3 + i)
    width = w_all.shape[2]
    for n in range(0, width, HALF):
        total = jnp.zeros((2 * ROWS, HALF), F32)
        for j in range(4):
            wide = w_all.shape[1] // 2
            w_rows = w_all[j // 2, (j % 2) * wide : (j % 2 + 1) * wide, n : n + HALF]
            total = total + mm(both(j), w_rows, 1, 0)
        hp_own[:, n : n + HALF] = total[0:ROWS]
        hp_out[:, n : n + HALF] = total[ROWS:]
    send(hp_out, hp_far, at_hp, partner)

    arrived(o_far, at_of)
    outputs = jnp.concatenate([o_masked[...], o_far[...]], axis=0)
    for j in range(4):
        product = mm(both(j), outputs, 0, 0)
        part[0, j] = product[:, 0:HALF]
        for i in range(4):
            part[1, i, j * ROWS : (j + 1) * ROWS] = product[i * ROWS : (i + 1) * ROWS, HALF:]

    first = [Scatter(i, part.at[i], part_out.at[i], half_in.at[i], full_in.at[i]) for i in range(2)]
    for scatter in first:
        scatter.start()

    arrived(hp_far, at_hp)
    hg_out[...] = jnp.where(live, hp_own[...] + hp_far[...], 0.0).astype(BF16)
    at_g = slots(4)
    for d in range(4):
        head = lax.rem(y + d, 4)
        peer = head * 2 + side
        give(peer == c, cols(hg_out, head), g_head.at[y], at_g + y, dev(c_=peer))

    for scatter in first:
        scatter.middle()

    held = []
    at_dq, at_dk, at_dv = slots(4), slots(8), slots(8)
    for t in (3, 2, 1, 0):
        n = 2 * ROWS * (t + 1)
        ct = shard[t]
        taken(ct == c, g_head.at[t], at_g + t)
        grad = g_head[t]
        delta = jnp.sum(grad.astype(F32) * o_head[t].astype(F32), axis=1, keepdims=True)
        probs = prob[t, :, 0:n]
        dprob = mm(grad, v_all[0:n], 1, 1)
        dscore = (probs * (dprob - delta)).astype(BF16)
        dq_out[t] = (mm(dscore, k_all[0:n], 1, 0) * scaling).astype(BF16)
        held.append((ct, dq_out.at[t], cols(dq_ref, y), at_dq + y))
        dk_part = mm(dscore, q_head[t], 0, 0)
        dv_part = mm(probs.astype(BF16), grad, 0, 0)
        if t == 3:
            dk_acc[...] = dk_part
            dv_acc[...] = dv_part
        else:
            dk_acc[0:n] += dk_part
            dv_acc[0:n] += dv_part
        for s in (2 * t + 1, 2 * t):
            at = slice(s * ROWS, (s + 1) * ROWS)
            dk_out[at] = (dk_acc[at] * scaling).astype(BF16)
            dv_out[at] = dv_acc[at].astype(BF16)
            held.append((jnp.int32(s), dk_out.at[at], cols(dk_ref.at[xl], y), at_dk + c))
            held.append((jnp.int32(s), dv_out.at[at], cols(dv_ref.at[xl], y), at_dv + c))

    def release(n):
        for _ in range(min(n, len(held))):
            peer, src, dst, index = held.pop(0)
            give(peer == c, src, dst, index, dev(c_=peer))

    second = [
        Scatter(1 - i, part2.at[i], part2_out.at[i], half2_in.at[i], full2_in.at[i])
        for i in range(2)
    ]
    for i in range(2):
        part2[i] = first[i].finish().reshape(part2.shape[1:])
        second[i].start()
    release(4)
    for i in range(2):
        second[i].middle()
    release(6)
    unit = xl * 4 + y
    for i in range(2):
        wg_ref[unit, :, i * HALF : (i + 1) * HALF] = second[i].finish().astype(BF16)
    at_x, at_y = slots(1), slots(8)
    other = dev(c_=y * 2 + 1 - xl)
    send(wg_ref.at[unit], wg_ref.at[unit], at_x, other)
    send(wg_ref.at[unit], wg_ref.at[unit], at_y, beside(1, 1))
    send(wg_ref.at[unit], wg_ref.at[unit], at_y + 1, beside(1, -1))
    release(4)
    unit2 = (1 - xl) * 4 + y
    arrived(wg_ref.at[unit2], at_x)
    send(wg_ref.at[unit2], wg_ref.at[unit2], at_y + 2, beside(1, 1))
    send(wg_ref.at[unit2], wg_ref.at[unit2], at_y + 3, beside(1, -1))
    release(4)
    below, above, far = (lax.rem(y + d, 4) for d in (3, 1, 2))
    columns = (xl * 4, (1 - xl) * 4)
    mid = ROWS // 2
    for i, column in enumerate(columns):
        low = wg_ref.at[column + below]
        arrived(low, at_y + 2 * i)
        send(low.at[0:mid], low.at[0:mid], at_y + 4 + 2 * i, beside(1, 1))
        high = wg_ref.at[column + above]
        arrived(high, at_y + 2 * i + 1)
        send(high.at[mid:], high.at[mid:], at_y + 5 + 2 * i, beside(1, -1))

    release(len(held))
    for h in range(4):
        taken(h * 2 + side == c, dq_ref.at[:, h * ROWS : (h + 1) * ROWS], at_dq + h)
    for s in range(8):
        at = slice((s // 2) * ROWS, (s // 2 + 1) * ROWS)
        taken(s == c, dk_ref.at[s % 2, :, at], at_dk + s)
        taken(s == c, dv_ref.at[s % 2, :, at], at_dv + s)
    for i, column in enumerate(columns):
        last = wg_ref.at[column + far]
        arrived(last.at[0:mid], at_y + 4 + 2 * i)
        arrived(last.at[mid:], at_y + 5 + 2 * i)

    for mine, copy in sent:
        if mine is None:
            copy.wait_send()
        else:
            pl.when(jnp.logical_not(mine))(copy.wait_send)
    assert next(send_index) <= ssem.shape[0] and next(recv_index) <= rsem.shape[0]


def write_out(dq_ref, dk_ref, dv_ref, wg_ref, dq_o, dk_o, dv_o, wg_o, dk_v, dv_v, wg_v, sem):
    copies = [pltpu.make_async_copy(dq_ref, dq_o, sem.at[8])]
    copies[0].start()
    for u in range(8):
        at = slice(u * ROWS, (u + 1) * ROWS)
        wg_v[at] = wg_ref[u].astype(F32)
        copies.append(pltpu.make_async_copy(wg_v.at[at], wg_o.at[at], sem.at[u]))
        copies[-1].start()
    for i, (src, mid, dst) in enumerate(((dk_ref, dk_v, dk_o), (dv_ref, dv_v, dv_o))):
        mid[...] = (src[0].astype(F32) + src[1].astype(F32)).astype(BF16)
        copies.append(pltpu.make_async_copy(mid, dst, sem.at[9 + i]))
        copies[-1].start()
    for copy in copies:
        copy.wait()


def per_device(queries, keys, values, out_grad, out_weight, slopes, counts, gaps):
    width = queries.shape[2]
    nz = lax.axis_size("tensor")
    vmem, hbm = pl.BlockSpec(memory_space=pltpu.VMEM), pl.BlockSpec(memory_space=pltpu.HBM)
    smem = pl.BlockSpec(memory_space=pltpu.SMEM)

    def v(dtype, *shape):
        return pltpu.VMEM(shape, dtype)

    dq, dk, dv, wg = pl.pallas_call(
        kernel,
        out_shape=(
            v(BF16, ROWS, width),
            v(BF16, 2, ROWS, width),
            v(BF16, 2, ROWS, width),
            v(BF16, 8, ROWS, width),
        ),
        in_specs=[smem, smem, vmem, hbm, hbm, hbm, hbm, hbm],
        out_specs=(vmem, vmem, vmem, vmem),
        scratch_shapes=[
            v(F32, 8, ROWS),
            v(F32, 8, 8, ROWS),
            v(BF16, 8 * ROWS, ROWS),
            v(BF16, 8 * ROWS, ROWS),
            v(BF16, 4, ROWS, ROWS),
            v(BF16, 4, ROWS, ROWS),
            v(BF16, nz, ROWS, width),
            v(BF16, 4, ROWS, width),
            v(BF16, 2, *out_weight.shape),
            v(F32, 4, ROWS, 8 * ROWS),
            v(BF16, 4, ROWS, ROWS),
            v(BF16, ROWS, width),
            v(BF16, ROWS, width),
            v(BF16, ROWS, width),
            v(F32, ROWS, width),
            v(F32, ROWS, width),
            v(F32, ROWS, width),
            v(BF16, ROWS, width),
            v(BF16, 4, ROWS, ROWS),
            v(F32, 8 * ROWS, ROWS),
            v(F32, 8 * ROWS, ROWS),
            v(BF16, 8 * ROWS, ROWS),
            v(BF16, 8 * ROWS, ROWS),
            v(F32, 2, 4, 4 * ROWS, HALF),
            v(BF16, 2, 4, 4 * ROWS, HALF),
            v(BF16, 2, 2, 2 * ROWS, HALF),
            v(BF16, 2, 2, 4 * ROWS, HALF),
            v(F32, 2, 4, ROWS, HALF),
            v(BF16, 2, 4, ROWS, HALF),
            v(BF16, 2, 2, ROWS // 2, HALF),
            v(BF16, 2, 2, ROWS, HALF),
            pltpu.SemaphoreType.DMA((144,)),
            pltpu.SemaphoreType.DMA((144,)),
        ],
        compiler_params=pltpu.CompilerParams(
            collective_id=0, has_side_effects=True, vmem_limit_bytes=62 << 20
        ),
        name="block_backward",
    )(
        slopes.reshape(1, -1), counts, gaps,
        queries[0], keys[0], values[0], out_grad[0], out_weight,
    )
    dq, dk, dv, wg = pl.pallas_call(
        write_out,
        out_shape=(
            jax.ShapeDtypeStruct((ROWS, width), BF16),
            jax.ShapeDtypeStruct((ROWS, width), BF16),
            jax.ShapeDtypeStruct((ROWS, width), BF16),
            jax.ShapeDtypeStruct((8 * ROWS, width), F32),
        ),
        in_specs=[vmem] * 4,
        out_specs=(hbm,) * 4,
        scratch_shapes=[
            v(BF16, ROWS, width),
            v(BF16, ROWS, width),
            v(F32, 8 * ROWS, width),
            pltpu.SemaphoreType.DMA((11,)),
        ],
        compiler_params=pltpu.CompilerParams(vmem_limit_bytes=12 << 20),
        name="write_out",
    )(dq, dk, dv, wg)
    return dq[None], dk[None], dv[None], wg


def solution(mesh):
    rows = P("fsdp", "context", "tensor")
    weight = P("fsdp", "tensor")
    placed = (rows, rows, rows, rows, weight, P("tensor"), P("fsdp", "context"))
    return jax.shard_map(
        per_device,
        mesh=mesh,
        in_specs=placed + (P("fsdp", "context"),),
        out_specs=(rows, rows, rows, weight),
        check_vma=False,
    )
```

```python
import itertools

import jax
import jax.numpy as jnp
from jax import lax
from jax.experimental import pallas as pl
from jax.experimental.pallas import tpu as pltpu
from jax.sharding import PartitionSpec as P

MESH = pl.DeviceIdType.MESH
F32, BF16 = jnp.float32, jnp.bfloat16
NEG = -1e30
ROWS = 128
HALF = 256


def mm(a, b, ca, cb):
    return lax.dot_general(a, b, (((ca,), (cb,)), ((), ())), preferred_element_type=F32)


def kernel(
    slopes_ref, counts_ref, gaps_ref, q_ref, k_ref, v_ref, g_ref, w_ref,
    dq_ref, dk_ref, dv_ref, wg_ref,
    gap_out, gap_all, k_all, v_all, q_head, g_head, g_all, g_far, w_all,
    prob, o_head, o_own, o_masked, o_far, hp_own, hp_out, hp_far, hg_out,
    dq_out, dk_acc, dv_acc, dk_out, dv_out,
    part, part_out, half_in, full_in, part2, part2_out, half2_in, full2_in,
    sem,
):
    c, z, f = lax.axis_index("context"), lax.axis_index("tensor"), lax.axis_index("fsdp")
    nz = g_all.shape[0]
    y, xl = lax.div(c, 2), lax.rem(c, 2)
    xh, core = lax.div(f, 2), lax.rem(f, 2)
    x = xh * 2 + xl
    place = (x, y)
    side = lax.rem(c + y, 2)
    scaling = ROWS ** (-0.5)
    count = counts_ref[...]
    even = lax.rem(y, 2) == 0

    def dev(c_=None, z_=None, f_=None):
        return {
            "context": c if c_ is None else c_,
            "tensor": z if z_ is None else z_,
            "fsdp": f if f_ is None else f_,
        }

    def beside(axis, step):
        if axis == 0:
            x2 = lax.rem(x + step + 4, 4)
            return dev(c_=y * 2 + lax.rem(x2, 2), f_=lax.div(x2, 2) * 2 + core)
        return dev(c_=lax.rem(y + step + 4, 4) * 2 + xl)

    right, left = dev(z_=lax.rem(z + 1, nz)), dev(z_=lax.rem(z + nz - 1, nz))
    partner = dev(f_=xh * 2 + 1 - core)
    across = dev(c_=y * 2 + 1 - xl, f_=(1 - xh) * 2 + core)

    semaphores = itertools.count()
    finals = []

    def slots(n):
        first = next(semaphores)
        for _ in range(n - 1):
            next(semaphores)
        return first

    def send(src, dst, index, where, group, mine=None):
        copy = pltpu.make_async_remote_copy(
            src_ref=src, dst_ref=dst, send_sem=sem.at[group],
            recv_sem=sem.at[index], device_id=where, device_id_type=MESH,
        )
        if mine is None:
            copy.start()
        else:
            pl.when(jnp.logical_not(mine))(copy.start)

    def give(mine, src, dst, index, where, group):
        send(src, dst, index, where, group, mine)
        pl.when(mine)(pltpu.make_async_copy(src, dst, sem.at[index]).start)

    def arrived(dst, index):
        pltpu.make_async_remote_copy(
            src_ref=dst, dst_ref=dst, send_sem=sem.at[index],
            recv_sem=sem.at[index], device_id=partner, device_id_type=MESH,
        ).wait_recv()

    def at_end(group, ref, when=None):
        finals.append((group, ref, when))

    def cols(ref, head):
        return ref.at[:, pl.ds(pl.multiple_of(head * ROWS, ROWS), ROWS)]

    def rows(ref, shard):
        return ref.at[pl.ds(pl.multiple_of(shard * ROWS, ROWS), ROWS)]

    lane8 = lax.broadcasted_iota(jnp.int32, (8, ROWS), 1)
    row8 = lax.broadcasted_iota(jnp.int32, (8, ROWS), 0)
    gap_out[...] = jnp.where(
        lane8 < jnp.broadcast_to(count, (8, ROWS)), jnp.broadcast_to(gaps_ref[...], (8, ROWS)), 0
    ).astype(F32)
    heads = lax.broadcasted_iota(jnp.int32, slopes_ref.shape, 1)
    slope = jnp.sum(jnp.where(heads == y, slopes_ref[...], 0.0), axis=1, keepdims=True)

    barrier = pltpu.get_barrier_semaphore()
    greeted = [dev(c_=lax.rem(c + d, 8)) for d in range(1, 8)] + [right, left, partner, across]
    for where in greeted:
        pl.semaphore_signal(barrier, inc=1, device_id=where, device_id_type=MESH)
    pl.semaphore_wait(barrier, len(greeted))

    at_gap, at_kvq, at_ring, at_far, at_w = slots(1), slots(4), slots(2 * nz), slots(1), slots(7)
    by_gap, by_kv, by_q, by_right, by_left, by_far, by_w = (slots(1) for _ in range(7))
    part_rows = ROWS // 2
    hops = nz // 2

    def piece(block, h):
        return g_all.at[block, h * part_rows : (h + 1) * part_rows]

    def to_partner(block, src):
        mine = lax.rem(lax.div(block, 2), 2) == core
        j = 2 * lax.div(block, 4) + lax.rem(block, 2)
        send(src, g_far.at[j], at_far, partner, by_far, mine)

    own_g = pltpu.make_async_copy(g_ref, g_all.at[z], sem.at[at_ring + 2 * nz - 1])
    own_g.start()
    for h in range(2):
        src = g_ref.at[h * part_rows : (h + 1) * part_rows]
        send(src, piece(z, h), at_ring + h, right, by_right)
        send(src, piece(z, h), at_ring + nz + h, left, by_left)
    pltpu.make_async_copy(gap_out, gap_all.at[c], sem.at[at_gap]).start()
    for d in range(1, 8):
        send(gap_out, gap_all.at[c], at_gap, dev(c_=lax.rem(c + d, 8)), by_gap)
    color = lax.rem(xl + y, 2)
    w_half = w_all.shape[1] // 2
    cuts = (0, 192, 384, 512)
    w_next = (beside(1, 1), beside(1, -1), dev(c_=y * 2 + 1 - xl))

    def w_piece(ref, half, i):
        at = pl.multiple_of(half * w_half + cuts[i], 64)
        return ref.at[pl.ds(at, cuts[i + 1] - cuts[i])]

    for i in range(3):
        there = w_piece(w_all.at[xh], 1 - color, i)
        send(w_piece(w_ref, 1 - color, i), there, at_w + i, across, by_w)
    for d in range(8):
        peer = lax.rem(c + d, 8)
        head = lax.div(peer, 2)
        for src, dst in ((k_ref, k_all), (v_ref, v_all)):
            if d == 0:
                pltpu.make_async_copy(cols(src, head), rows(dst, c), sem.at[at_kvq + y]).start()
            else:
                send(cols(src, head), rows(dst, c), at_kvq + y, dev(c_=peer), by_kv)
        if d < 4:
            head = lax.rem(y + d, 4)
            peer = head * 2 + side
            give(peer == c, cols(q_ref, head), q_head.at[y], at_kvq + y, dev(c_=peer), by_q)
    to_partner(z, g_ref)
    own_w = pltpu.make_async_copy(w_ref, w_all.at[xh], sem.at[at_w + 6])
    own_w.start()
    at_end(by_gap, gap_all.at[0:7])
    at_end(by_kv, w_all.at[0, 0:448])
    for by in (by_right, by_left):
        at_end(by, w_all.at[0, 0 : part_rows * (2 * hops - 1)])
    at_end(by_far, g_far)
    at_end(by_w, w_all.at[0])

    def at_end_heads(by):
        at_end(by, o_head.at[0:3], even)
        at_end(by, o_head, jnp.logical_not(even))

    at_end_heads(by_q)

    last = 2 * (hops - 1)

    def ring(k):
        d, h = k // 2 + 1, k % 2
        for way, (where, step, base) in enumerate(
            ((right, nz - d, at_ring), (left, d, at_ring + nz))
        ):
            block = lax.rem(z + step, nz)
            half = way if k == last else h
            arrived(piece(block, half), base + k)
            if d + 1 < hops or (d + 1 == hops and h == way):
                after = min(k + 2, last)
                by = (by_right, by_left)[way]
                send(piece(block, half), piece(block, half), base + after, where, by)
            if h == 1:
                to_partner(block, g_all.at[block])
        if k == last:
            to_partner(lax.rem(z + hops, nz), g_all.at[lax.rem(z + hops, nz)])

    def w_pass(i):
        theirs = w_piece(w_all.at[1 - xh], color, i)
        arrived(theirs, at_w + i)
        send(theirs, theirs, at_w + 3 + i, w_next[i], by_w)

    ring(0)

    arrived(gap_all, at_gap)
    gaps8 = jnp.zeros((8, ROWS), F32)
    before = jnp.zeros((8, ROWS), F32)
    for s in range(8):
        gaps8 = jnp.where(row8 == s, gap_all[s], gaps8)
        before = before + jnp.where(row8 > s, gap_all[s], 0.0)
    r128 = lax.broadcasted_iota(jnp.int32, (ROWS, ROWS), 0)
    l128 = lax.broadcasted_iota(jnp.int32, (ROWS, ROWS), 1)
    upto = (r128 <= l128).astype(BF16)
    offs8 = mm(gaps8.astype(BF16), upto, 1, 0) + jnp.sum(before, axis=1, keepdims=True)
    k_offset = jnp.concatenate([offs8[s : s + 1] for s in range(8)], axis=1)
    k_valid = jnp.concatenate([gaps8[s : s + 1] for s in range(8)], axis=1) > 0.0

    at_o, by_o = slots(1), slots(1)
    at_end_heads(by_o)
    shard = [2 * t + lax.rem(xl + t, 2) for t in range(4)]

    def forward(t):
        n = 2 * ROWS * (t + 1)
        ct = shard[t]
        arrived(k_all.at[0 : 5 * ROWS], at_kvq + t)
        q_gaps = gap_all[ct][0:1]
        q_before = jnp.zeros((1, ROWS), F32)
        for s in range(2 * t + 1):
            q_before = q_before + gap_all[s][0:1] * (s < ct).astype(F32)
        q_offset = jnp.sum(
            jnp.where(l128 <= r128, jnp.broadcast_to(q_gaps, (ROWS, ROWS)), 0.0)
            + jnp.broadcast_to(q_before, (ROWS, ROWS)),
            axis=1, keepdims=True,
        )
        logits = mm(q_head[t], k_all[0:n], 1, 1) * scaling
        logits = logits - slope * (q_offset - k_offset[:, 0:n])
        q_slot = ct * ROWS + lax.broadcasted_iota(jnp.int32, (ROWS, n), 0)
        k_slot = lax.broadcasted_iota(jnp.int32, (ROWS, n), 1)
        allowed = jnp.logical_and(k_valid[:, 0:n], k_slot <= q_slot)
        logits = jnp.where(allowed, logits, NEG)
        peak = jnp.max(logits, axis=1, keepdims=True)
        weight = jnp.where(allowed, jnp.exp(logits - peak), 0.0)
        probs = weight * (1.0 / jnp.sum(weight, axis=1, keepdims=True))
        prob[t, :, 0:n] = probs
        o_head[t] = mm(probs.astype(BF16), v_all[0:n], 1, 0).astype(BF16)
        give(ct == c, o_head.at[t], cols(o_own, y), at_o, dev(c_=ct), by_o)

    ring(1)
    w_pass(0)
    ring(2)
    ring(3)
    ring(4)
    w_pass(1)
    ring(5)
    forward(0)
    forward(1)
    ring(6)
    w_pass(2)
    forward(2)
    forward(3)
    own_g.wait()

    at_of, at_hp, by_of, by_hp = (slots(1) for _ in range(4))
    arrived(o_own, at_o)
    live = lax.broadcasted_iota(jnp.int32, o_own.shape, 0) < jnp.broadcast_to(count, o_own.shape)
    o_masked[...] = jnp.where(live, o_own[...], jnp.zeros_like(o_own))
    send(o_masked, o_far, at_of, partner, by_of)
    at_end(by_of, o_masked)
    arrived(g_far, at_far)

    def both(j):
        mine = g_all[4 * (j // 2) + 2 * core + j % 2]
        return jnp.concatenate([mine, g_far[j]], axis=0)

    class Scatter:
        def __init__(self, axis, terms, out, half, full, by):
            self.axis, self.terms, self.out, self.half, self.full = axis, terms, out, half, full
            self.at, self.by = slots(6), by
            mid = terms.shape[1] // 2
            self.low, self.high = slice(0, mid), slice(mid, 2 * mid)
            p = place[axis]
            self.own = p
            self.far, self.up, self.down = (lax.rem(p + d, 4) for d in (2, 1, 3))
            self.after, self.behind = beside(axis, 1), beside(axis, -1)

        def pass_on(self, group, at, way, more=None):
            terms = self.terms[group, at]
            if more is not None:
                terms = terms + more.astype(F32)
            self.out[group, at] = terms.astype(BF16)
            index = self.at + 2 + 2 * way + (more is not None)
            where = (self.after, self.behind)[way]
            send(self.out.at[group, at], self.full.at[way, at], index, where, self.by)

        def start(self):
            self.out[self.far] = self.terms[self.far].astype(BF16)
            far = self.out.at[self.far]
            send(far.at[self.low], self.half.at[0], self.at, self.after, self.by)
            send(far.at[self.high], self.half.at[1], self.at + 1, self.behind, self.by)

        def more(self):
            self.pass_on(self.up, self.high, 0)
            self.pass_on(self.down, self.low, 1)

        def middle(self):
            arrived(self.half.at[0], self.at)
            self.pass_on(self.up, self.low, 0, self.half[0])
            arrived(self.half.at[1], self.at + 1)
            self.pass_on(self.down, self.high, 1, self.half[1])

        def finish(self):
            for way in range(2):
                arrived(self.full.at[way, self.low], self.at + 2 + 2 * way)
                arrived(self.full.at[way, self.high], self.at + 3 + 2 * way)
            return self.terms[self.own] + self.full[0].astype(F32) + self.full[1].astype(F32)

    own_w.wait()
    for i in range(3):
        arrived(w_piece(w_all.at[1 - xh], 1 - color, i), at_w + 3 + i)
    width = w_all.shape[2]
    for n in range(0, width, HALF):
        total = jnp.zeros((2 * ROWS, HALF), F32)
        for j in range(4):
            wide = w_all.shape[1] // 2
            w_rows = w_all[j // 2, (j % 2) * wide : (j % 2 + 1) * wide, n : n + HALF]
            total = total + mm(both(j), w_rows, 1, 0)
        hp_own[:, n : n + HALF] = total[0:ROWS]
        hp_out[:, n : n + HALF] = total[ROWS:]
    send(hp_out, hp_far, at_hp, partner, by_hp)
    at_end(by_hp, hp_out)

    arrived(o_far, at_of)
    outputs = jnp.concatenate([o_masked[...], o_far[...]], axis=0)
    for j in range(4):
        product = mm(both(j), outputs, 0, 0)
        part[0, j] = product[:, 0:HALF]
        for i in range(4):
            part[1, i, j * ROWS : (j + 1) * ROWS] = product[i * ROWS : (i + 1) * ROWS, HALF:]

    by_first, by_second = slots(2), slots(1)
    for i in range(2):
        at_end(by_first + i, part_out.at[i, 0:3])
    at_end(by_second, part2_out.at[:, 0:3])
    first = [
        Scatter(i, part.at[i], part_out.at[i], half_in.at[i], full_in.at[i], by_first + i)
        for i in range(2)
    ]
    for scatter in first:
        scatter.start()

    arrived(hp_far, at_hp)
    hg_out[...] = jnp.where(live, hp_own[...] + hp_far[...], 0.0).astype(BF16)
    at_g, by_g = slots(1), slots(1)
    at_end_heads(by_g)
    for d in range(4):
        head = lax.rem(y + d, 4)
        peer = head * 2 + side
        give(peer == c, cols(hg_out, head), g_head.at[y], at_g, dev(c_=peer), by_g)

    for scatter in first:
        scatter.more()
    for scatter in first:
        scatter.middle()

    held = []
    at_dq, at_dk, at_dv, by_dq, by_dkv = (slots(1) for _ in range(5))
    at_end_heads(by_dq)
    at_end(by_dkv, w_all.at[0, 0:448])
    arrived(g_head, at_g)
    for t in (3, 2, 1, 0):
        n = 2 * ROWS * (t + 1)
        ct = shard[t]
        grad = g_head[t]
        delta = jnp.sum(grad.astype(F32) * o_head[t].astype(F32), axis=1, keepdims=True)
        probs = prob[t, :, 0:n]
        dprob = mm(grad, v_all[0:n], 1, 1)
        dscore = (probs * (dprob - delta)).astype(BF16)
        dq_out[t] = (mm(dscore, k_all[0:n], 1, 0) * scaling).astype(BF16)
        dk_part = mm(dscore, q_head[t], 0, 0)
        dv_part = mm(probs.astype(BF16), grad, 0, 0)
        if t == 3:
            dk_acc[...] = dk_part
            dv_acc[...] = dv_part
        else:
            dk_acc[0:n] += dk_part
            dv_acc[0:n] += dv_part
        for s in (2 * t + 1, 2 * t):
            at = slice(s * ROWS, (s + 1) * ROWS)
            dk_out[at] = (dk_acc[at] * scaling).astype(BF16)
            dv_out[at] = dv_acc[at].astype(BF16)

    for d in range(4):
        t = lax.rem(y + d, 4)
        held.append((2 * t + lax.rem(xl + t, 2), dq_out.at[t], cols(dq_ref, y), at_dq, by_dq))
    for d in range(8):
        s = lax.rem(c + d, 8)
        held.append((s, rows(dk_out, s), cols(dk_ref.at[xl], y), at_dk, by_dkv))
        held.append((s, rows(dv_out, s), cols(dv_ref.at[xl], y), at_dv, by_dkv))

    def release(n):
        for _ in range(min(n, len(held))):
            peer, src, dst, index, by = held.pop(0)
            give(peer == c, src, dst, index, dev(c_=peer), by)

    release(6)
    second = [
        Scatter(1 - i, part2.at[i], part2_out.at[i], half2_in.at[i], full2_in.at[i], by_second)
        for i in range(2)
    ]
    for i in range(2):
        part2[i] = first[i].finish().reshape(part2.shape[1:])
        second[i].start()
        second[i].more()
    release(5)
    for i in range(2):
        second[i].middle()
    release(4)
    at_x, at_y, by_all = slots(2), slots(16), slots(1)
    at_end(by_all, wg_ref.at[0:7])
    near, back = beside(1, 1), beside(1, -1)
    other = dev(c_=y * 2 + 1 - xl)
    below, above, far = (lax.rem(y + d, 4) for d in (3, 1, 2))
    columns = (xl * 4, (1 - xl) * 4)
    mid = ROWS // 2

    def unit(column, place_y, i):
        return wg_ref.at[column + place_y, :, i * HALF : (i + 1) * HALF]

    for i in range(2):
        mine = unit(columns[0], y, i)
        mine[...] = second[i].finish().astype(BF16)
        send(mine, mine, at_x + i, other, by_all)
        send(mine, mine, at_y + 2 * i, near, by_all)
        send(mine, mine, at_y + 2 * i + 1, back, by_all)
    release(3)
    for i in range(2):
        mine = unit(columns[1], y, i)
        arrived(mine, at_x + i)
        send(mine, mine, at_y + 4 + 2 * i, near, by_all)
        send(mine, mine, at_y + 4 + 2 * i + 1, back, by_all)
    release(len(held))
    for j, column in enumerate(columns):
        for i in range(2):
            low = unit(column, below, i)
            arrived(low, at_y + 4 * j + 2 * i)
            send(low.at[0:mid], low.at[0:mid], at_y + 8 + 4 * j + 2 * i, near, by_all)
            high = unit(column, above, i)
            arrived(high, at_y + 4 * j + 2 * i + 1)
            send(high.at[mid:], high.at[mid:], at_y + 9 + 4 * j + 2 * i, back, by_all)

    arrived(dq_ref, at_dq)
    arrived(dk_ref, at_dk)
    arrived(dv_ref, at_dv)
    for j, column in enumerate(columns):
        for i in range(2):
            end = unit(column, far, i)
            arrived(end.at[0:mid], at_y + 8 + 4 * j + 2 * i)
            arrived(end.at[mid:], at_y + 9 + 4 * j + 2 * i)

    for group, ref, when in finals:
        wait = pltpu.make_async_remote_copy(
            src_ref=ref, dst_ref=ref, send_sem=sem.at[group],
            recv_sem=sem.at[group], device_id=partner, device_id_type=MESH,
        ).wait_send
        if when is None:
            wait()
        else:
            pl.when(when)(wait)
    assert next(semaphores) == sem.shape[0], next(semaphores)


def write_out(dq_ref, dk_ref, dv_ref, wg_ref, dq_o, dk_o, dv_o, wg_o, dk_v, dv_v, wg_v, sem):
    copies = [pltpu.make_async_copy(dq_ref, dq_o, sem.at[8])]
    copies[0].start()
    for u in range(8):
        at = slice(u * ROWS, (u + 1) * ROWS)
        wg_v[at] = wg_ref[u].astype(F32)
        copies.append(pltpu.make_async_copy(wg_v.at[at], wg_o.at[at], sem.at[u]))
        copies[-1].start()
    for i, (src, mid, dst) in enumerate(((dk_ref, dk_v, dk_o), (dv_ref, dv_v, dv_o))):
        mid[...] = (src[0].astype(F32) + src[1].astype(F32)).astype(BF16)
        copies.append(pltpu.make_async_copy(mid, dst, sem.at[9 + i]))
        copies[-1].start()
    for copy in copies:
        copy.wait()


def per_device(queries, keys, values, out_grad, out_weight, slopes, counts, gaps):
    width = queries.shape[2]
    nz = lax.axis_size("tensor")
    vmem, hbm = pl.BlockSpec(memory_space=pltpu.VMEM), pl.BlockSpec(memory_space=pltpu.HBM)

    def v(dtype, *shape):
        return pltpu.VMEM(shape, dtype)

    dq, dk, dv, wg = pl.pallas_call(
        kernel,
        out_shape=(
            v(BF16, ROWS, width),
            v(BF16, 2, ROWS, width),
            v(BF16, 2, ROWS, width),
            v(BF16, 8, ROWS, width),
        ),
        in_specs=[vmem, vmem, vmem, hbm, hbm, hbm, hbm, hbm],
        out_specs=(vmem, vmem, vmem, vmem),
        scratch_shapes=[
            v(F32, 8, ROWS),
            v(F32, 8, 8, ROWS),
            v(BF16, 8 * ROWS, ROWS),
            v(BF16, 8 * ROWS, ROWS),
            v(BF16, 4, ROWS, ROWS),
            v(BF16, 4, ROWS, ROWS),
            v(BF16, nz, ROWS, width),
            v(BF16, 4, ROWS, width),
            v(BF16, 2, *out_weight.shape),
            v(F32, 4, ROWS, 8 * ROWS),
            v(BF16, 4, ROWS, ROWS),
            v(BF16, ROWS, width),
            v(BF16, ROWS, width),
            v(BF16, ROWS, width),
            v(F32, ROWS, width),
            v(F32, ROWS, width),
            v(F32, ROWS, width),
            v(BF16, ROWS, width),
            v(BF16, 4, ROWS, ROWS),
            v(F32, 8 * ROWS, ROWS),
            v(F32, 8 * ROWS, ROWS),
            v(BF16, 8 * ROWS, ROWS),
            v(BF16, 8 * ROWS, ROWS),
            v(F32, 2, 4, 4 * ROWS, HALF),
            v(BF16, 2, 4, 4 * ROWS, HALF),
            v(BF16, 2, 2, 2 * ROWS, HALF),
            v(BF16, 2, 2, 4 * ROWS, HALF),
            v(F32, 2, 4, ROWS, HALF),
            v(BF16, 2, 4, ROWS, HALF),
            v(BF16, 2, 2, ROWS // 2, HALF),
            v(BF16, 2, 2, ROWS, HALF),
            pltpu.SemaphoreType.DMA((95,)),
        ],
        compiler_params=pltpu.CompilerParams(
            collective_id=0, has_side_effects=True, vmem_limit_bytes=62 << 20
        ),
        name="block_backward",
    )(
        slopes.reshape(1, -1), counts, gaps,
        queries[0], keys[0], values[0], out_grad[0], out_weight,
    )
    dq, dk, dv, wg = pl.pallas_call(
        write_out,
        out_shape=(
            jax.ShapeDtypeStruct((ROWS, width), BF16),
            jax.ShapeDtypeStruct((ROWS, width), BF16),
            jax.ShapeDtypeStruct((ROWS, width), BF16),
            jax.ShapeDtypeStruct((8 * ROWS, width), F32),
        ),
        in_specs=[vmem] * 4,
        out_specs=(hbm,) * 4,
        scratch_shapes=[
            v(BF16, ROWS, width),
            v(BF16, ROWS, width),
            v(F32, 8 * ROWS, width),
            pltpu.SemaphoreType.DMA((11,)),
        ],
        compiler_params=pltpu.CompilerParams(vmem_limit_bytes=12 << 20),
        name="write_out",
    )(dq, dk, dv, wg)
    return dq[None], dk[None], dv[None], wg


def solution(mesh):
    rows = P("fsdp", "context", "tensor")
    weight = P("fsdp", "tensor")
    placed = (rows, rows, rows, rows, weight, P("tensor"), P("fsdp", "context"))
    return jax.shard_map(
        per_device,
        mesh=mesh,
        in_specs=placed + (P("fsdp", "context"),),
        out_specs=(rows, rows, rows, weight),
        check_vma=False,
    )
```

```python
import itertools

import jax
import jax.numpy as jnp
from jax import lax
from jax.experimental import pallas as pl
from jax.experimental.pallas import tpu as pltpu
from jax.sharding import PartitionSpec as P

MESH = pl.DeviceIdType.MESH
F32, BF16 = jnp.float32, jnp.bfloat16
NEG = -1e30
ROWS = 128
HALF = 256
AXES = (0, 1, 0, 1)
PAIRS = ((0, 1), (2, 3))


def mm(a, b, ca, cb):
    return lax.dot_general(a, b, (((ca,), (cb,)), ((), ())), preferred_element_type=F32)


def kernel(
    slopes_ref, counts_ref, gaps_ref, q_ref, k_ref, v_ref, g_ref, w_ref,
    dq_ref, dk_ref, dv_ref, wg_ref,
    gap_out, gap_all, k_all, v_all, q_head, g_head, g_all, g_far, w_all,
    prob, o_head, o_own, o_masked, o_far, hp_own, hp_out, hp_far, hg_out,
    dq_out, dk_acc, dv_acc, dkv_out, dkv_in, dkv_sum,
    part, part_out, half_in, full_in, part2, part2_out, full2_in,
    sem,
):
    c, z, f = lax.axis_index("context"), lax.axis_index("tensor"), lax.axis_index("fsdp")
    nz = g_all.shape[0]
    y, xl = lax.div(c, 2), lax.rem(c, 2)
    xh, core = lax.div(f, 2), lax.rem(f, 2)
    x = xh * 2 + xl
    place = (x, y)
    side = lax.rem(c + y, 2)
    scaling = ROWS ** (-0.5)
    count = counts_ref[...]
    even = lax.rem(y, 2) == 0

    def dev(c_=None, z_=None, f_=None):
        return {
            "context": c if c_ is None else c_,
            "tensor": z if z_ is None else z_,
            "fsdp": f if f_ is None else f_,
        }

    def beside(axis, step):
        if axis == 0:
            x2 = lax.rem(x + step + 4, 4)
            return dev(c_=y * 2 + lax.rem(x2, 2), f_=lax.div(x2, 2) * 2 + core)
        return dev(c_=lax.rem(y + step + 4, 4) * 2 + xl)

    right, left = dev(z_=lax.rem(z + 1, nz)), dev(z_=lax.rem(z + nz - 1, nz))
    partner = dev(f_=xh * 2 + 1 - core)
    across = dev(c_=y * 2 + 1 - xl, f_=(1 - xh) * 2 + core)

    semaphores = itertools.count()
    finals = []

    def slots(n):
        first = next(semaphores)
        for _ in range(n - 1):
            next(semaphores)
        return first

    def send(src, dst, index, where, group, mine=None):
        copy = pltpu.make_async_remote_copy(
            src_ref=src, dst_ref=dst, send_sem=sem.at[group],
            recv_sem=sem.at[index], device_id=where, device_id_type=MESH,
        )
        if mine is None:
            copy.start()
        else:
            pl.when(jnp.logical_not(mine))(copy.start)

    def give(mine, src, dst, index, where, group):
        send(src, dst, index, where, group, mine)
        pl.when(mine)(pltpu.make_async_copy(src, dst, sem.at[index]).start)

    def arrived(dst, index):
        pltpu.make_async_remote_copy(
            src_ref=dst, dst_ref=dst, send_sem=sem.at[index],
            recv_sem=sem.at[index], device_id=partner, device_id_type=MESH,
        ).wait_recv()

    def at_end(group, ref, when=None):
        finals.append((group, ref, when))

    def cols(ref, head):
        return ref.at[:, pl.ds(pl.multiple_of(head * ROWS, ROWS), ROWS)]

    def rows(ref, shard):
        return ref.at[pl.ds(pl.multiple_of(shard * ROWS, ROWS), ROWS)]

    lane8 = lax.broadcasted_iota(jnp.int32, (8, ROWS), 1)
    row8 = lax.broadcasted_iota(jnp.int32, (8, ROWS), 0)
    gap_out[...] = jnp.where(
        lane8 < jnp.broadcast_to(count, (8, ROWS)), jnp.broadcast_to(gaps_ref[...], (8, ROWS)), 0
    ).astype(F32)
    heads = lax.broadcasted_iota(jnp.int32, slopes_ref.shape, 1)
    slope = jnp.sum(jnp.where(heads == y, slopes_ref[...], 0.0), axis=1, keepdims=True)

    barrier = pltpu.get_barrier_semaphore()
    greeted = [dev(c_=lax.rem(c + d, 8)) for d in range(1, 8)] + [right, left, partner, across]
    greeted.append(dev(f_=(1 - xh) * 2 + core))
    for where in greeted:
        pl.semaphore_signal(barrier, inc=1, device_id=where, device_id_type=MESH)
    pl.semaphore_wait(barrier, len(greeted))

    at_gap, at_kvq, at_ring, at_far, at_w = slots(1), slots(4), slots(2 * nz), slots(1), slots(7)
    by_gap, by_kv, by_q, by_right, by_left, by_far, by_w = (slots(1) for _ in range(7))
    part_rows = ROWS // 2
    hops = nz // 2

    def piece(block, h):
        return g_all.at[block, h * part_rows : (h + 1) * part_rows]

    def to_partner(block, src):
        mine = lax.rem(lax.div(block, 2), 2) == core
        j = 2 * lax.div(block, 4) + lax.rem(block, 2)
        send(src, g_far.at[j], at_far, partner, by_far, mine)

    own_g = pltpu.make_async_copy(g_ref, g_all.at[z], sem.at[at_ring + 2 * nz - 1])
    own_g.start()
    for h in range(2):
        src = g_ref.at[h * part_rows : (h + 1) * part_rows]
        send(src, piece(z, h), at_ring + h, right, by_right)
        send(src, piece(z, h), at_ring + nz + h, left, by_left)
    pltpu.make_async_copy(gap_out, gap_all.at[c], sem.at[at_gap]).start()
    for d in range(1, 8):
        send(gap_out, gap_all.at[c], at_gap, dev(c_=lax.rem(c + d, 8)), by_gap)
    color = lax.rem(xl + y, 2)
    w_half = w_all.shape[1] // 2
    cuts = (0, 192, 384, 512)
    w_next = (beside(1, 1), beside(1, -1), dev(c_=y * 2 + 1 - xl))

    def w_piece(ref, half, i):
        at = pl.multiple_of(half * w_half + cuts[i], 64)
        return ref.at[pl.ds(at, cuts[i + 1] - cuts[i])]

    for i in range(3):
        there = w_piece(w_all.at[xh], 1 - color, i)
        send(w_piece(w_ref, 1 - color, i), there, at_w + i, across, by_w)
    for d in range(8):
        peer = lax.rem(c + d, 8)
        head = lax.div(peer, 2)
        for src, dst in ((k_ref, k_all), (v_ref, v_all)):
            if d == 0:
                pltpu.make_async_copy(cols(src, head), rows(dst, c), sem.at[at_kvq + y]).start()
            else:
                send(cols(src, head), rows(dst, c), at_kvq + y, dev(c_=peer), by_kv)
        if d < 4:
            head = lax.rem(y + d, 4)
            peer = head * 2 + side
            give(peer == c, cols(q_ref, head), q_head.at[y], at_kvq + y, dev(c_=peer), by_q)
    to_partner(z, g_ref)
    own_w = pltpu.make_async_copy(w_ref, w_all.at[xh], sem.at[at_w + 6])
    own_w.start()
    at_end(by_gap, gap_all.at[0:7])
    at_end(by_kv, w_all.at[0, 0:448])
    for by in (by_right, by_left):
        at_end(by, w_all.at[0, 0 : part_rows * (2 * hops - 1)])
    at_end(by_far, g_far)
    at_end(by_w, w_all.at[0])

    def at_end_heads(by):
        at_end(by, o_head.at[0:3], even)
        at_end(by, o_head, jnp.logical_not(even))

    at_end_heads(by_q)

    last = 2 * (hops - 1)

    def ring(k):
        d, h = k // 2 + 1, k % 2
        for way, (where, step, base) in enumerate(
            ((right, nz - d, at_ring), (left, d, at_ring + nz))
        ):
            block = lax.rem(z + step, nz)
            half = way if k == last else h
            arrived(piece(block, half), base + k)
            if d + 1 < hops or (d + 1 == hops and h == way):
                after = min(k + 2, last)
                by = (by_right, by_left)[way]
                send(piece(block, half), piece(block, half), base + after, where, by)
            if h == 1:
                to_partner(block, g_all.at[block])
        if k == last:
            to_partner(lax.rem(z + hops, nz), g_all.at[lax.rem(z + hops, nz)])

    def w_pass(i):
        theirs = w_piece(w_all.at[1 - xh], color, i)
        arrived(theirs, at_w + i)
        send(theirs, theirs, at_w + 3 + i, w_next[i], by_w)

    ring(0)

    arrived(gap_all, at_gap)
    gaps8 = jnp.zeros((8, ROWS), F32)
    before = jnp.zeros((8, ROWS), F32)
    for s in range(8):
        gaps8 = jnp.where(row8 == s, gap_all[s], gaps8)
        before = before + jnp.where(row8 > s, gap_all[s], 0.0)
    r128 = lax.broadcasted_iota(jnp.int32, (ROWS, ROWS), 0)
    l128 = lax.broadcasted_iota(jnp.int32, (ROWS, ROWS), 1)
    upto = (r128 <= l128).astype(BF16)
    offs8 = mm(gaps8.astype(BF16), upto, 1, 0) + jnp.sum(before, axis=1, keepdims=True)
    k_offset = jnp.concatenate([offs8[s : s + 1] for s in range(8)], axis=1)
    k_valid = jnp.concatenate([gaps8[s : s + 1] for s in range(8)], axis=1) > 0.0

    at_o, by_o = slots(1), slots(1)
    at_end_heads(by_o)
    shard = [2 * t + lax.rem(xl + t, 2) for t in range(4)]

    def forward(t):
        n = 2 * ROWS * (t + 1)
        ct = shard[t]
        arrived(k_all.at[0 : 5 * ROWS], at_kvq + t)
        q_gaps = gap_all[ct][0:1]
        q_before = jnp.zeros((1, ROWS), F32)
        for s in range(2 * t + 1):
            q_before = q_before + gap_all[s][0:1] * (s < ct).astype(F32)
        q_offset = jnp.sum(
            jnp.where(l128 <= r128, jnp.broadcast_to(q_gaps, (ROWS, ROWS)), 0.0)
            + jnp.broadcast_to(q_before, (ROWS, ROWS)),
            axis=1, keepdims=True,
        )
        logits = mm(q_head[t], k_all[0:n], 1, 1) * scaling
        logits = logits - slope * (q_offset - k_offset[:, 0:n])
        q_slot = ct * ROWS + lax.broadcasted_iota(jnp.int32, (ROWS, n), 0)
        k_slot = lax.broadcasted_iota(jnp.int32, (ROWS, n), 1)
        allowed = jnp.logical_and(k_valid[:, 0:n], k_slot <= q_slot)
        logits = jnp.where(allowed, logits, NEG)
        peak = jnp.max(logits, axis=1, keepdims=True)
        weight = jnp.where(allowed, jnp.exp(logits - peak), 0.0)
        probs = weight * (1.0 / jnp.sum(weight, axis=1, keepdims=True))
        prob[t, :, 0:n] = probs
        o_head[t] = mm(probs.astype(BF16), v_all[0:n], 1, 0).astype(BF16)
        give(ct == c, o_head.at[t], cols(o_own, y), at_o, dev(c_=ct), by_o)

    ring(1)
    w_pass(0)
    ring(2)
    ring(3)
    ring(4)
    w_pass(1)
    ring(5)
    forward(0)
    forward(1)
    forward(2)
    forward(3)
    w_pass(2)
    ring(6)
    own_g.wait()

    at_of, at_hp, by_of, by_hp = (slots(1) for _ in range(4))
    arrived(o_own, at_o)
    live = lax.broadcasted_iota(jnp.int32, o_own.shape, 0) < jnp.broadcast_to(count, o_own.shape)
    o_masked[...] = jnp.where(live, o_own[...], jnp.zeros_like(o_own))
    send(o_masked, o_far, at_of, partner, by_of)
    at_end(by_of, o_masked)
    arrived(g_far, at_far)

    def both(j):
        mine = g_all[4 * (j // 2) + 2 * core + j % 2]
        return jnp.concatenate([mine, g_far[j]], axis=0)

    class Scatter:
        def __init__(self, axis, terms, out, half, full, by):
            self.axis, self.terms, self.out, self.half, self.full = axis, terms, out, half, full
            self.at, self.by = slots(6), by
            mid = terms.shape[1] // 2
            self.low, self.high = slice(0, mid), slice(mid, 2 * mid)
            p = place[axis]
            self.own = p
            self.far, self.up, self.down = (lax.rem(p + d, 4) for d in (2, 1, 3))
            self.after, self.behind = beside(axis, 1), beside(axis, -1)

        def pass_on(self, group, at, way, more=None):
            terms = self.terms[group, at]
            if more is not None:
                terms = terms + more.astype(F32)
            self.out[group, at] = terms.astype(BF16)
            index = self.at + 2 + 2 * way + (more is not None)
            where = (self.after, self.behind)[way]
            send(self.out.at[group, at], self.full.at[way, at], index, where, self.by)

        def start(self):
            self.out[self.far] = self.terms[self.far].astype(BF16)
            far = self.out.at[self.far]
            send(far.at[self.low], self.half.at[0], self.at, self.after, self.by)
            send(far.at[self.high], self.half.at[1], self.at + 1, self.behind, self.by)

        def more(self):
            self.pass_on(self.up, self.high, 0)
            self.pass_on(self.down, self.low, 1)

        def middle(self):
            arrived(self.half.at[0], self.at)
            self.pass_on(self.up, self.low, 0, self.half[0])
            arrived(self.half.at[1], self.at + 1)
            self.pass_on(self.down, self.high, 1, self.half[1])

        def finish(self):
            for way in range(2):
                arrived(self.full.at[way, self.low], self.at + 2 + 2 * way)
                arrived(self.full.at[way, self.high], self.at + 3 + 2 * way)
            return self.terms[self.own] + self.full[0].astype(F32) + self.full[1].astype(F32)

    arrived(o_far, at_of)
    outputs = jnp.concatenate([o_masked[...], o_far[...]], axis=0)
    for j in range(4):
        product = mm(both(j), outputs, 0, 0)
        for n, axis in enumerate(AXES):
            chunk = product[:, n * ROWS : (n + 1) * ROWS]
            if axis == 0:
                part[n, j] = chunk
            else:
                for i in range(4):
                    part[n, i, j * ROWS : (j + 1) * ROWS] = chunk[i * ROWS : (i + 1) * ROWS]

    class Exchange:
        def __init__(self, axis, terms, out, full, by):
            self.axis, self.terms, self.out, self.full = axis, terms, out, full
            self.at, self.by, self.own = slots(1), by, place[axis]

        def start(self):
            for d in (2, 1, 3):
                group = lax.rem(self.own + d, 4)
                self.out[group] = self.terms[group].astype(BF16)
                where = beside(self.axis, d)
                send(self.out.at[group], self.full.at[d - 1], self.at, where, self.by)

        def finish(self):
            arrived(self.full, self.at)
            return self.terms[self.own] + sum(self.full[d].astype(F32) for d in range(3))

    by_first, by_second = slots(4), slots(1)
    for n in range(4):
        at_end(by_first + n, part_out.at[n, 0:3])
    at_end(by_second, part2_out.at[:, 0:3])
    first, second = [], []
    for n, axis in enumerate(AXES):
        bufs = (part.at[n], part_out.at[n], half_in.at[n], full_in.at[n])
        first.append(Scatter(axis, *bufs, by_first + n))
        bufs = (part2.at[n], part2_out.at[n], full2_in.at[n])
        second.append(Exchange(1 - axis, *bufs, by_second))

    def each(chunks, *calls):
        for call in calls:
            for n in chunks:
                call(n)

    one, two = PAIRS
    each(one, lambda n: first[n].start())
    each(one, lambda n: first[n].more())

    own_w.wait()
    for i in range(3):
        arrived(w_piece(w_all.at[1 - xh], 1 - color, i), at_w + 3 + i)
    width = w_all.shape[2]
    for n in range(0, width, HALF):
        total = jnp.zeros((2 * ROWS, HALF), F32)
        for j in range(4):
            wide = w_all.shape[1] // 2
            w_rows = w_all[j // 2, (j % 2) * wide : (j % 2 + 1) * wide, n : n + HALF]
            total = total + mm(both(j), w_rows, 1, 0)
        hp_own[:, n : n + HALF] = total[0:ROWS]
        hp_out[:, n : n + HALF] = total[ROWS:]
    send(hp_out, hp_far, at_hp, partner, by_hp)
    at_end(by_hp, hp_out)

    arrived(hp_far, at_hp)
    hg_out[...] = jnp.where(live, hp_own[...] + hp_far[...], 0.0).astype(BF16)
    at_g, by_g = slots(1), slots(1)
    at_end_heads(by_g)
    for d in range(4):
        head = lax.rem(y + d, 4)
        peer = head * 2 + side
        give(peer == c, cols(hg_out, head), g_head.at[y], at_g, dev(c_=peer), by_g)

    each(two, lambda n: first[n].start())
    each(one, lambda n: first[n].middle())
    each(two, lambda n: first[n].more())

    def halfway(n):
        part2[n] = first[n].finish().reshape(part2.shape[1:])
        second[n].start()

    each(two, lambda n: first[n].middle())
    each(one, halfway)

    held = []
    at_dq, at_dk, at_dv, at_swap, by_dq, by_dk, by_dv, by_swap = (slots(1) for _ in range(8))
    at_end_heads(by_dq)
    at_end(by_dk, o_head.at[0:3])
    at_end(by_dv, o_head.at[0:3])
    at_end(by_swap, dkv_in)
    arrived(g_head, at_g)
    for t in (3, 2, 1, 0):
        n = 2 * ROWS * (t + 1)
        ct = shard[t]
        grad = g_head[t]
        delta = jnp.sum(grad.astype(F32) * o_head[t].astype(F32), axis=1, keepdims=True)
        probs = prob[t, :, 0:n]
        dprob = mm(grad, v_all[0:n], 1, 1)
        dscore = (probs * (dprob - delta)).astype(BF16)
        dq_out[t] = (mm(dscore, k_all[0:n], 1, 0) * scaling).astype(BF16)
        dk_part = mm(dscore, q_head[t], 0, 0)
        dv_part = mm(probs.astype(BF16), grad, 0, 0)
        if t == 3:
            dk_acc[...] = dk_part
            dv_acc[...] = dv_part
        else:
            dk_acc[0:n] += dk_part
            dv_acc[0:n] += dv_part
        for s in (2 * t + 1, 2 * t):
            at = slice(s * ROWS, (s + 1) * ROWS)
            dkv_out[s % 2, 0, t] = (dk_acc[at] * scaling).astype(BF16)
            dkv_out[s % 2, 1, t] = dv_acc[at].astype(BF16)

    for d in range(4):
        t = lax.rem(y + d, 4)
        held.append((2 * t + lax.rem(xl + t, 2), dq_out.at[t], cols(dq_ref, y), at_dq, by_dq))
    def release(n):
        for _ in range(min(n, len(held))):
            peer, src, dst, index, by = held.pop(0)
            give(peer == c, src, dst, index, dev(c_=peer), by)

    other = dev(c_=y * 2 + 1 - xl)

    def swap(i):
        src = dkv_out.at[1 - xl, i // 2, 2 * (i % 2) : 2 * (i % 2) + 2]
        dst = dkv_in.at[i // 2, 2 * (i % 2) : 2 * (i % 2) + 2]
        send(src, dst, at_swap, other, by_swap)


    def add_swapped():
        arrived(dkv_in, at_swap)
        for t in range(4):
            at = pl.ds(pl.multiple_of((2 * t + xl) * ROWS, ROWS), ROWS)
            dkv_sum[0, t] = (dk_acc[at] * scaling + dkv_in[0, t].astype(F32)).astype(BF16)
            dkv_sum[1, t] = (dv_acc[at] + dkv_in[1, t].astype(F32)).astype(BF16)
        for d in range(4):
            t = lax.rem(y + d, 4)
            there = 2 * t + xl
            held.append((there, dkv_sum.at[0, t], cols(dk_ref, y), at_dk, by_dk))
            held.append((there, dkv_sum.at[1, t], cols(dv_ref, y), at_dv, by_dv))


    at_x, at_y, by_all = slots(2), slots(16), slots(1)
    at_end(by_all, wg_ref.at[0:7])
    near, back = beside(1, 1), beside(1, -1)
    below, above, far = (lax.rem(y + d, 4) for d in (3, 1, 2))
    columns = (xl * 4, (1 - xl) * 4)
    mid = ROWS // 2

    def unit(column, place_y, i):
        return wg_ref.at[column + place_y, :, i * HALF : (i + 1) * HALF]

    def gather(i):
        mine = unit(columns[0], y, i)
        for n in PAIRS[i]:
            at = slice(n * ROWS, (n + 1) * ROWS)
            wg_ref[columns[0] + y, :, at] = second[n].finish().astype(BF16)
        send(mine, mine, at_x + i, other, by_all)
        send(mine, mine, at_y + 2 * i, near, by_all)
        send(mine, mine, at_y + 2 * i + 1, back, by_all)

    def pass_x(i):
        mine = unit(columns[1], y, i)
        arrived(mine, at_x + i)
        send(mine, mine, at_y + 4 + 2 * i, near, by_all)
        send(mine, mine, at_y + 4 + 2 * i + 1, back, by_all)

    def pass_y(j, i):
        low = unit(columns[j], below, i)
        arrived(low, at_y + 4 * j + 2 * i)
        send(low.at[0:mid], low.at[0:mid], at_y + 8 + 4 * j + 2 * i, near, by_all)
        high = unit(columns[j], above, i)
        arrived(high, at_y + 4 * j + 2 * i + 1)
        send(high.at[mid:], high.at[mid:], at_y + 9 + 4 * j + 2 * i, back, by_all)

    def pass_x_last():
        low = unit(columns[0], below, 1)
        arrived(low, at_y + 2)
        send(low.at[0:mid], low.at[0:mid], at_y + 10, near, by_all)
        send(low, low, at_y + 6, other, by_all)
        high = unit(columns[0], above, 1)
        arrived(high, at_y + 3)
        send(high.at[mid:], high.at[mid:], at_y + 11, back, by_all)
        send(high, high, at_y + 7, other, by_all)

    release(2)
    swap(0)
    each(two, halfway)
    release(2)
    gather(0)
    swap(1)
    gather(1)
    swap(2)
    pass_x(0)
    swap(3)
    pass_y(0, 0)
    pass_x_last()
    pass_y(1, 0)
    add_swapped()
    release(len(held))
    end = unit(columns[0], far, 1)
    arrived(end.at[0:mid], at_y + 10)
    arrived(end.at[mid:], at_y + 11)
    send(end, end, at_y + 14, other, by_all)
    arrived(dq_ref, at_dq)
    arrived(dk_ref, at_dk)
    arrived(dv_ref, at_dv)
    for j, column in enumerate(columns):
        end = unit(column, far, 0)
        arrived(end.at[0:mid], at_y + 8 + 4 * j)
        arrived(end.at[mid:], at_y + 9 + 4 * j)
    for place_y, index in ((y, at_x + 1), (below, at_y + 6), (above, at_y + 7), (far, at_y + 14)):
        arrived(unit(columns[1], place_y, 1), index)

    for group, ref, when in finals:
        wait = pltpu.make_async_remote_copy(
            src_ref=ref, dst_ref=ref, send_sem=sem.at[group],
            recv_sem=sem.at[group], device_id=partner, device_id_type=MESH,
        ).wait_send
        if when is None:
            wait()
        else:
            pl.when(when)(wait)
    used = next(semaphores)
    assert used == sem.shape[0], used


def write_out(dq_ref, dk_ref, dv_ref, wg_ref, dq_o, dk_o, dv_o, wg_o, wg_v, sem):
    copies = []
    for u in range(8):
        at = slice(u * ROWS, (u + 1) * ROWS)
        wg_v[at] = wg_ref[u].astype(F32)
        copies.append(pltpu.make_async_copy(wg_v.at[at], wg_o.at[at], sem.at[u]))
        copies[-1].start()
    for i, (src, dst) in enumerate(((dq_ref, dq_o), (dk_ref, dk_o), (dv_ref, dv_o))):
        copies.append(pltpu.make_async_copy(src, dst, sem.at[8 + i]))
        copies[-1].start()
    for copy in copies:
        copy.wait()


def per_device(queries, keys, values, out_grad, out_weight, slopes, counts, gaps):
    width = queries.shape[2]
    nz = lax.axis_size("tensor")
    vmem, hbm = pl.BlockSpec(memory_space=pltpu.VMEM), pl.BlockSpec(memory_space=pltpu.HBM)

    def v(dtype, *shape):
        return pltpu.VMEM(shape, dtype)

    dq, dk, dv, wg = pl.pallas_call(
        kernel,
        out_shape=(
            v(BF16, ROWS, width),
            v(BF16, ROWS, width),
            v(BF16, ROWS, width),
            v(BF16, 8, ROWS, width),
        ),
        in_specs=[vmem, vmem, vmem, hbm, hbm, hbm, hbm, hbm],
        out_specs=(vmem, vmem, vmem, vmem),
        scratch_shapes=[
            v(F32, 8, ROWS),
            v(F32, 8, 8, ROWS),
            v(BF16, 8 * ROWS, ROWS),
            v(BF16, 8 * ROWS, ROWS),
            v(BF16, 4, ROWS, ROWS),
            v(BF16, 4, ROWS, ROWS),
            v(BF16, nz, ROWS, width),
            v(BF16, 4, ROWS, width),
            v(BF16, 2, *out_weight.shape),
            v(F32, 4, ROWS, 8 * ROWS),
            v(BF16, 4, ROWS, ROWS),
            v(BF16, ROWS, width),
            v(BF16, ROWS, width),
            v(BF16, ROWS, width),
            v(F32, ROWS, width),
            v(F32, ROWS, width),
            v(F32, ROWS, width),
            v(BF16, ROWS, width),
            v(BF16, 4, ROWS, ROWS),
            v(F32, 8 * ROWS, ROWS),
            v(F32, 8 * ROWS, ROWS),
            v(BF16, 2, 2, 4, ROWS, ROWS),
            v(BF16, 2, 4, ROWS, ROWS),
            v(BF16, 2, 4, ROWS, ROWS),
            v(F32, 4, 4, 4 * ROWS, ROWS),
            v(BF16, 4, 4, 4 * ROWS, ROWS),
            v(BF16, 4, 2, 2 * ROWS, ROWS),
            v(BF16, 4, 2, 4 * ROWS, ROWS),
            v(F32, 4, 4, ROWS, ROWS),
            v(BF16, 4, 4, ROWS, ROWS),
            v(BF16, 4, 3, ROWS, ROWS),
            pltpu.SemaphoreType.DMA((104,)),
        ],
        compiler_params=pltpu.CompilerParams(
            collective_id=0, has_side_effects=True, vmem_limit_bytes=62 << 20
        ),
        name="block_backward",
    )(
        slopes.reshape(1, -1), counts, gaps,
        queries[0], keys[0], values[0], out_grad[0], out_weight,
    )
    dq, dk, dv, wg = pl.pallas_call(
        write_out,
        out_shape=(
            jax.ShapeDtypeStruct((ROWS, width), BF16),
            jax.ShapeDtypeStruct((ROWS, width), BF16),
            jax.ShapeDtypeStruct((ROWS, width), BF16),
            jax.ShapeDtypeStruct((8 * ROWS, width), F32),
        ),
        in_specs=[vmem] * 4,
        out_specs=(hbm,) * 4,
        scratch_shapes=[
            v(F32, 8 * ROWS, width),
            pltpu.SemaphoreType.DMA((11,)),
        ],
        compiler_params=pltpu.CompilerParams(vmem_limit_bytes=12 << 20),
        name="write_out",
    )(dq, dk, dv, wg)
    return dq[None], dk[None], dv[None], wg


def solution(mesh):
    rows = P("fsdp", "context", "tensor")
    weight = P("fsdp", "tensor")
    placed = (rows, rows, rows, rows, weight, P("tensor"), P("fsdp", "context"))
    return jax.shard_map(
        per_device,
        mesh=mesh,
        in_specs=placed + (P("fsdp", "context"),),
        out_specs=(rows, rows, rows, weight),
        check_vma=False,
    )
```

```python
import itertools

import jax
import jax.numpy as jnp
from jax import lax
from jax.experimental import pallas as pl
from jax.experimental.pallas import tpu as pltpu
from jax.sharding import PartitionSpec as P

MESH = pl.DeviceIdType.MESH
F32, BF16 = jnp.float32, jnp.bfloat16
NEG = -1e30
ROWS = 128
HALF = 256
AXES = (0, 1, 0, 1)
PAIRS = ((0, 1), (2, 3))


def mm(a, b, ca, cb):
    return lax.dot_general(a, b, (((ca,), (cb,)), ((), ())), preferred_element_type=F32)


def kernel(
    slopes_ref, counts_ref, gaps_ref, q_ref, k_ref, v_ref, g_ref, w_ref,
    dq_ref, dk_ref, dv_ref, wg_ref,
    gap_out, gap_all, k_all, v_all, q_head, g_head, g_all, g_far, w_all,
    prob, o_head, o_own, o_masked, o_far, hp_own, hp_out, hp_far, hg_out,
    dq_out, dk_acc, dv_acc, dkv_out, dkv_in, dkv_sum,
    part, part_out, half_in, full_in, part2, part2_out, full2_in,
    sem,
):
    c, z, f = lax.axis_index("context"), lax.axis_index("tensor"), lax.axis_index("fsdp")
    nz = g_all.shape[0]
    y, xl = lax.div(c, 2), lax.rem(c, 2)
    xh, core = lax.div(f, 2), lax.rem(f, 2)
    x = xh * 2 + xl
    place = (x, y)
    side = lax.rem(c + y, 2)
    scaling = ROWS ** (-0.5)
    count = counts_ref[...]
    even = lax.rem(y, 2) == 0

    def dev(c_=None, z_=None, f_=None):
        return {
            "context": c if c_ is None else c_,
            "tensor": z if z_ is None else z_,
            "fsdp": f if f_ is None else f_,
        }

    def beside(axis, step):
        if axis == 0:
            x2 = lax.rem(x + step + 4, 4)
            return dev(c_=y * 2 + lax.rem(x2, 2), f_=lax.div(x2, 2) * 2 + core)
        return dev(c_=lax.rem(y + step + 4, 4) * 2 + xl)

    right, left = dev(z_=lax.rem(z + 1, nz)), dev(z_=lax.rem(z + nz - 1, nz))
    partner = dev(f_=xh * 2 + 1 - core)
    across = dev(c_=y * 2 + 1 - xl, f_=(1 - xh) * 2 + core)

    semaphores = itertools.count()
    finals = []

    def slots(n):
        first = next(semaphores)
        for _ in range(n - 1):
            next(semaphores)
        return first

    def send(src, dst, index, where, group, mine=None):
        copy = pltpu.make_async_remote_copy(
            src_ref=src, dst_ref=dst, send_sem=sem.at[group],
            recv_sem=sem.at[index], device_id=where, device_id_type=MESH,
        )
        if mine is None:
            copy.start()
        else:
            pl.when(jnp.logical_not(mine))(copy.start)

    def give(mine, src, dst, index, where, group):
        send(src, dst, index, where, group, mine)
        pl.when(mine)(pltpu.make_async_copy(src, dst, sem.at[index]).start)

    def arrived(dst, index):
        pltpu.make_async_remote_copy(
            src_ref=dst, dst_ref=dst, send_sem=sem.at[index],
            recv_sem=sem.at[index], device_id=partner, device_id_type=MESH,
        ).wait_recv()

    def at_end(group, ref, when=None):
        finals.append((group, ref, when))

    def cols(ref, head):
        return ref.at[:, pl.ds(pl.multiple_of(head * ROWS, ROWS), ROWS)]

    def rows(ref, shard):
        return ref.at[pl.ds(pl.multiple_of(shard * ROWS, ROWS), ROWS)]

    lane8 = lax.broadcasted_iota(jnp.int32, (8, ROWS), 1)
    row8 = lax.broadcasted_iota(jnp.int32, (8, ROWS), 0)
    gap_out[...] = jnp.where(
        lane8 < jnp.broadcast_to(count, (8, ROWS)), jnp.broadcast_to(gaps_ref[...], (8, ROWS)), 0
    ).astype(F32)
    heads = lax.broadcasted_iota(jnp.int32, slopes_ref.shape, 1)
    slope = jnp.sum(jnp.where(heads == y, slopes_ref[...], 0.0), axis=1, keepdims=True)

    barrier = pltpu.get_barrier_semaphore()
    greeted = [dev(c_=lax.rem(c + d, 8)) for d in range(1, 8)] + [right, left, partner, across]
    greeted.append(dev(f_=(1 - xh) * 2 + core))
    for where in greeted:
        pl.semaphore_signal(barrier, inc=1, device_id=where, device_id_type=MESH)
    pl.semaphore_wait(barrier, len(greeted))

    at_gap, at_kvq, at_ring, at_far, at_w = slots(1), slots(4), slots(2 * nz), slots(1), slots(7)
    by_gap, by_kv, by_q, by_right, by_left, by_far, by_w = (slots(1) for _ in range(7))
    part_rows = ROWS // 2
    hops = nz // 2

    def piece(block, h):
        return g_all.at[block, h * part_rows : (h + 1) * part_rows]

    def to_partner(block, src):
        mine = lax.rem(lax.div(block, 2), 2) == core
        j = 2 * lax.div(block, 4) + lax.rem(block, 2)
        send(src, g_far.at[j], at_far, partner, by_far, mine)

    own_g = pltpu.make_async_copy(g_ref, g_all.at[z], sem.at[at_ring + 2 * nz - 1])
    own_g.start()
    for h in range(2):
        src = g_ref.at[h * part_rows : (h + 1) * part_rows]
        send(src, piece(z, h), at_ring + h, right, by_right)
        send(src, piece(z, h), at_ring + nz + h, left, by_left)
    pltpu.make_async_copy(gap_out, gap_all.at[c], sem.at[at_gap]).start()
    for d in range(1, 8):
        send(gap_out, gap_all.at[c], at_gap, dev(c_=lax.rem(c + d, 8)), by_gap)
    color = lax.rem(xl + y, 2)
    w_half = w_all.shape[1] // 2
    cuts = (0, 192, 384, 512)
    w_next = (beside(1, 1), beside(1, -1), dev(c_=y * 2 + 1 - xl))

    def w_piece(ref, half, i):
        at = pl.multiple_of(half * w_half + cuts[i], 64)
        return ref.at[pl.ds(at, cuts[i + 1] - cuts[i])]

    for i in range(3):
        there = w_piece(w_all.at[xh], 1 - color, i)
        send(w_piece(w_ref, 1 - color, i), there, at_w + i, across, by_w)
    for d in range(8):
        peer = lax.rem(c + d, 8)
        head = lax.div(peer, 2)
        for src, dst in ((k_ref, k_all), (v_ref, v_all)):
            if d == 0:
                pltpu.make_async_copy(cols(src, head), rows(dst, c), sem.at[at_kvq + y]).start()
            else:
                send(cols(src, head), rows(dst, c), at_kvq + y, dev(c_=peer), by_kv)
        if d < 4:
            head = lax.rem(y + d, 4)
            peer = head * 2 + side
            give(peer == c, cols(q_ref, head), q_head.at[y], at_kvq + y, dev(c_=peer), by_q)
    to_partner(z, g_ref)
    own_w = pltpu.make_async_copy(w_ref, w_all.at[xh], sem.at[at_w + 6])
    own_w.start()
    at_end(by_gap, gap_all.at[0:7])
    at_end(by_kv, w_all.at[0, 0:448])
    for by in (by_right, by_left):
        at_end(by, w_all.at[0, 0 : part_rows * (2 * hops - 1)])
    at_end(by_far, g_far)
    at_end(by_w, w_all.at[0])

    def at_end_heads(by):
        at_end(by, o_head.at[0:3], even)
        at_end(by, o_head, jnp.logical_not(even))

    at_end_heads(by_q)

    last = 2 * (hops - 1)

    def ring(k):
        d, h = k // 2 + 1, k % 2
        for way, (where, step, base) in enumerate(
            ((right, nz - d, at_ring), (left, d, at_ring + nz))
        ):
            block = lax.rem(z + step, nz)
            half = way if k == last else h
            arrived(piece(block, half), base + k)
            if d + 1 < hops or (d + 1 == hops and h == way):
                after = min(k + 2, last)
                by = (by_right, by_left)[way]
                send(piece(block, half), piece(block, half), base + after, where, by)
            if h == 1:
                to_partner(block, g_all.at[block])
        if k == last:
            to_partner(lax.rem(z + hops, nz), g_all.at[lax.rem(z + hops, nz)])

    def w_pass(i):
        theirs = w_piece(w_all.at[1 - xh], color, i)
        arrived(theirs, at_w + i)
        send(theirs, theirs, at_w + 3 + i, w_next[i], by_w)

    ring(0)

    arrived(gap_all, at_gap)
    gaps8 = jnp.zeros((8, ROWS), F32)
    before = jnp.zeros((8, ROWS), F32)
    for s in range(8):
        gaps8 = jnp.where(row8 == s, gap_all[s], gaps8)
        before = before + jnp.where(row8 > s, gap_all[s], 0.0)
    r128 = lax.broadcasted_iota(jnp.int32, (ROWS, ROWS), 0)
    l128 = lax.broadcasted_iota(jnp.int32, (ROWS, ROWS), 1)
    upto = (r128 <= l128).astype(BF16)
    offs8 = mm(gaps8.astype(BF16), upto, 1, 0) + jnp.sum(before, axis=1, keepdims=True)
    k_offset = jnp.concatenate([offs8[s : s + 1] for s in range(8)], axis=1)
    k_valid = jnp.concatenate([gaps8[s : s + 1] for s in range(8)], axis=1) > 0.0

    at_o, by_o = slots(1), slots(1)
    at_end_heads(by_o)
    shard = [2 * t + lax.rem(xl + t, 2) for t in range(4)]

    def forward(t):
        n = 2 * ROWS * (t + 1)
        ct = shard[t]
        arrived(k_all.at[0 : 5 * ROWS], at_kvq + t)
        q_gaps = gap_all[ct][0:1]
        q_before = jnp.zeros((1, ROWS), F32)
        for s in range(2 * t + 1):
            q_before = q_before + gap_all[s][0:1] * (s < ct).astype(F32)
        q_offset = jnp.sum(
            jnp.where(l128 <= r128, jnp.broadcast_to(q_gaps, (ROWS, ROWS)), 0.0)
            + jnp.broadcast_to(q_before, (ROWS, ROWS)),
            axis=1, keepdims=True,
        )
        logits = mm(q_head[t], k_all[0:n], 1, 1) * scaling
        logits = logits - slope * (q_offset - k_offset[:, 0:n])
        q_slot = ct * ROWS + lax.broadcasted_iota(jnp.int32, (ROWS, n), 0)
        k_slot = lax.broadcasted_iota(jnp.int32, (ROWS, n), 1)
        allowed = jnp.logical_and(k_valid[:, 0:n], k_slot <= q_slot)
        logits = jnp.where(allowed, logits, NEG)
        peak = jnp.max(logits, axis=1, keepdims=True)
        weight = jnp.where(allowed, jnp.exp(logits - peak), 0.0)
        probs = weight * (1.0 / jnp.sum(weight, axis=1, keepdims=True))
        prob[t, :, 0:n] = probs
        o_head[t] = mm(probs.astype(BF16), v_all[0:n], 1, 0).astype(BF16)
        give(ct == c, o_head.at[t], cols(o_own, y), at_o, dev(c_=ct), by_o)

    ring(1)
    w_pass(0)
    ring(2)
    ring(3)
    ring(4)
    forward(0)
    forward(1)
    ring(5)
    forward(2)
    forward(3)
    w_pass(1)
    w_pass(2)
    ring(6)
    own_g.wait()

    at_of, at_hp, by_of, by_hp = (slots(1) for _ in range(4))
    arrived(o_own, at_o)
    live = lax.broadcasted_iota(jnp.int32, o_own.shape, 0) < jnp.broadcast_to(count, o_own.shape)
    o_masked[...] = jnp.where(live, o_own[...], jnp.zeros_like(o_own))
    send(o_masked, o_far, at_of, partner, by_of)
    at_end(by_of, o_masked)
    arrived(g_far, at_far)

    def both(j):
        mine = g_all[4 * (j // 2) + 2 * core + j % 2]
        return jnp.concatenate([mine, g_far[j]], axis=0)

    class Scatter:
        def __init__(self, axis, terms, out, half, full, by):
            self.axis, self.terms, self.out, self.half, self.full = axis, terms, out, half, full
            self.at, self.by = slots(6), by
            mid = terms.shape[1] // 2
            self.low, self.high = slice(0, mid), slice(mid, 2 * mid)
            p = place[axis]
            self.own = p
            self.far, self.up, self.down = (lax.rem(p + d, 4) for d in (2, 1, 3))
            self.after, self.behind = beside(axis, 1), beside(axis, -1)

        def pass_on(self, group, at, way, more=None):
            terms = self.terms[group, at]
            if more is not None:
                terms = terms + more.astype(F32)
            self.out[group, at] = terms.astype(BF16)
            index = self.at + 2 + 2 * way + (more is not None)
            where = (self.after, self.behind)[way]
            send(self.out.at[group, at], self.full.at[way, at], index, where, self.by)

        def start(self):
            self.out[self.far] = self.terms[self.far].astype(BF16)
            far = self.out.at[self.far]
            send(far.at[self.low], self.half.at[0], self.at, self.after, self.by)
            send(far.at[self.high], self.half.at[1], self.at + 1, self.behind, self.by)

        def more(self):
            self.pass_on(self.up, self.high, 0)
            self.pass_on(self.down, self.low, 1)

        def middle(self):
            arrived(self.half.at[0], self.at)
            self.pass_on(self.up, self.low, 0, self.half[0])
            arrived(self.half.at[1], self.at + 1)
            self.pass_on(self.down, self.high, 1, self.half[1])

        def finish(self):
            for way in range(2):
                arrived(self.full.at[way, self.low], self.at + 2 + 2 * way)
                arrived(self.full.at[way, self.high], self.at + 3 + 2 * way)
            return self.terms[self.own] + self.full[0].astype(F32) + self.full[1].astype(F32)

    arrived(o_far, at_of)
    outputs = jnp.concatenate([o_masked[...], o_far[...]], axis=0)
    for j in range(4):
        product = mm(both(j), outputs, 0, 0)
        for n, axis in enumerate(AXES):
            chunk = product[:, n * ROWS : (n + 1) * ROWS]
            if axis == 0:
                part[n, j] = chunk
            else:
                for i in range(4):
                    part[n, i, j * ROWS : (j + 1) * ROWS] = chunk[i * ROWS : (i + 1) * ROWS]

    class Exchange:
        def __init__(self, axis, terms, out, full, by):
            self.axis, self.terms, self.out, self.full = axis, terms, out, full
            self.at, self.by, self.own = slots(1), by, place[axis]

        def start(self):
            for d in (2, 1, 3):
                group = lax.rem(self.own + d, 4)
                self.out[group] = self.terms[group].astype(BF16)
                where = beside(self.axis, d)
                send(self.out.at[group], self.full.at[d - 1], self.at, where, self.by)

        def finish(self):
            arrived(self.full, self.at)
            return self.terms[self.own] + sum(self.full[d].astype(F32) for d in range(3))

    by_first, by_second = slots(4), slots(1)
    for n in range(4):
        at_end(by_first + n, part_out.at[n, 0:3])
    at_end(by_second, part2_out.at[:, 0:3])
    first, second = [], []
    for n, axis in enumerate(AXES):
        bufs = (part.at[n], part_out.at[n], half_in.at[n], full_in.at[n])
        first.append(Scatter(axis, *bufs, by_first + n))
        bufs = (part2.at[n], part2_out.at[n], full2_in.at[n])
        second.append(Exchange(1 - axis, *bufs, by_second))

    def each(chunks, *calls):
        for call in calls:
            for n in chunks:
                call(n)

    one, two = PAIRS
    each(one, lambda n: first[n].start())
    each(one, lambda n: first[n].more())

    own_w.wait()
    for i in range(3):
        arrived(w_piece(w_all.at[1 - xh], 1 - color, i), at_w + 3 + i)
    width = w_all.shape[2]
    for n in range(0, width, HALF):
        total = jnp.zeros((2 * ROWS, HALF), F32)
        for j in range(4):
            wide = w_all.shape[1] // 2
            w_rows = w_all[j // 2, (j % 2) * wide : (j % 2 + 1) * wide, n : n + HALF]
            total = total + mm(both(j), w_rows, 1, 0)
        hp_own[:, n : n + HALF] = total[0:ROWS]
        hp_out[:, n : n + HALF] = total[ROWS:]
    send(hp_out, hp_far, at_hp, partner, by_hp)
    at_end(by_hp, hp_out)

    arrived(hp_far, at_hp)
    hg_out[...] = jnp.where(live, hp_own[...] + hp_far[...], 0.0).astype(BF16)
    at_g, by_g = slots(1), slots(1)
    at_end_heads(by_g)
    for d in range(4):
        head = lax.rem(y + d, 4)
        peer = head * 2 + side
        give(peer == c, cols(hg_out, head), g_head.at[y], at_g, dev(c_=peer), by_g)

    each(two, lambda n: first[n].start())
    each(one, lambda n: first[n].middle())
    each(two, lambda n: first[n].more())

    def halfway(n):
        part2[n] = first[n].finish().reshape(part2.shape[1:])
        second[n].start()

    held = []
    at_dq, at_dk, at_dv, by_dq, by_dk, by_dv, by_swap = (slots(1) for _ in range(7))
    at_swap = slots(2)
    at_end_heads(by_dq)
    at_end(by_dk, o_head.at[0:3])
    at_end(by_dv, o_head.at[0:3])
    at_end(by_swap, dkv_in)
    arrived(g_head, at_g)
    for t in (3, 2, 1, 0):
        n = 2 * ROWS * (t + 1)
        ct = shard[t]
        grad = g_head[t]
        delta = jnp.sum(grad.astype(F32) * o_head[t].astype(F32), axis=1, keepdims=True)
        probs = prob[t, :, 0:n]
        dprob = mm(grad, v_all[0:n], 1, 1)
        dscore = (probs * (dprob - delta)).astype(BF16)
        dq_out[t] = (mm(dscore, k_all[0:n], 1, 0) * scaling).astype(BF16)
        dk_part = mm(dscore, q_head[t], 0, 0)
        dv_part = mm(probs.astype(BF16), grad, 0, 0)
        if t == 3:
            dk_acc[...] = dk_part
            dv_acc[...] = dv_part
        else:
            dk_acc[0:n] += dk_part
            dv_acc[0:n] += dv_part
        for s in (2 * t + 1, 2 * t):
            at = slice(s * ROWS, (s + 1) * ROWS)
            dkv_out[s % 2, 0, t] = (dk_acc[at] * scaling).astype(BF16)
            dkv_out[s % 2, 1, t] = dv_acc[at].astype(BF16)

    for d in range(4):
        t = lax.rem(y + d, 4)
        held.append((2 * t + lax.rem(xl + t, 2), dq_out.at[t], cols(dq_ref, y), at_dq, by_dq))
    def release(n):
        for _ in range(min(n, len(held))):
            peer, src, dst, index, by = held.pop(0)
            give(peer == c, src, dst, index, dev(c_=peer), by)

    other = dev(c_=y * 2 + 1 - xl)

    def swap(i):
        src = dkv_out.at[1 - xl, i // 2, 2 * (i % 2) : 2 * (i % 2) + 2]
        dst = dkv_in.at[i // 2, 2 * (i % 2) : 2 * (i % 2) + 2]
        send(src, dst, at_swap + i // 2, other, by_swap)


    def add_swapped(i):
        arrived(dkv_in.at[i], at_swap + i)
        for t in range(4):
            at = pl.ds(pl.multiple_of((2 * t + xl) * ROWS, ROWS), ROWS)
            mine = dk_acc[at] * scaling if i == 0 else dv_acc[at]
            dkv_sum[i, t] = (mine + dkv_in[i, t].astype(F32)).astype(BF16)
        dst, index, by = ((dk_ref, at_dk, by_dk), (dv_ref, at_dv, by_dv))[i]
        for d in range(4):
            t = lax.rem(y + d, 4)
            held.append((2 * t + xl, dkv_sum.at[i, t], cols(dst, y), index, by))


    at_x, at_y, by_all = slots(2), slots(16), slots(1)
    at_end(by_all, wg_ref.at[0:7])
    near, back = beside(1, 1), beside(1, -1)
    below, above, far = (lax.rem(y + d, 4) for d in (3, 1, 2))
    columns = (xl * 4, (1 - xl) * 4)
    mid = ROWS // 2

    def unit(column, place_y, i):
        return wg_ref.at[column + place_y, :, i * HALF : (i + 1) * HALF]

    def gather(i):
        mine = unit(columns[0], y, i)
        for n in PAIRS[i]:
            at = slice(n * ROWS, (n + 1) * ROWS)
            wg_ref[columns[0] + y, :, at] = second[n].finish().astype(BF16)
        send(mine, mine, at_x + i, other, by_all)
        send(mine, mine, at_y + 2 * i, near, by_all)
        send(mine, mine, at_y + 2 * i + 1, back, by_all)

    def pass_x(i):
        mine = unit(columns[1], y, i)
        arrived(mine, at_x + i)
        send(mine, mine, at_y + 4 + 2 * i, near, by_all)
        send(mine, mine, at_y + 4 + 2 * i + 1, back, by_all)

    def pass_y(j, i):
        low = unit(columns[j], below, i)
        arrived(low, at_y + 4 * j + 2 * i)
        send(low.at[0:mid], low.at[0:mid], at_y + 8 + 4 * j + 2 * i, near, by_all)
        high = unit(columns[j], above, i)
        arrived(high, at_y + 4 * j + 2 * i + 1)
        send(high.at[mid:], high.at[mid:], at_y + 9 + 4 * j + 2 * i, back, by_all)

    def pass_x_last():
        low = unit(columns[0], below, 1)
        arrived(low, at_y + 2)
        send(low.at[0:mid], low.at[0:mid], at_y + 10, near, by_all)
        send(low, low, at_y + 6, other, by_all)
        high = unit(columns[0], above, 1)
        arrived(high, at_y + 3)
        send(high.at[mid:], high.at[mid:], at_y + 11, back, by_all)
        send(high, high, at_y + 7, other, by_all)

    each(two, lambda n: first[n].middle())
    each(one, halfway)
    swap(0)
    each(two, halfway)
    gather(0)
    swap(1)
    release(2)
    gather(1)
    swap(2)
    release(2)
    pass_x(0)
    swap(3)
    add_swapped(0)
    release(4)
    pass_y(0, 0)
    pass_x_last()
    pass_y(1, 0)
    add_swapped(1)
    release(4)
    end = unit(columns[0], far, 1)
    arrived(end.at[0:mid], at_y + 10)
    arrived(end.at[mid:], at_y + 11)
    send(end, end, at_y + 14, other, by_all)
    arrived(dq_ref, at_dq)
    arrived(dk_ref, at_dk)
    arrived(dv_ref, at_dv)
    for j, column in enumerate(columns):
        end = unit(column, far, 0)
        arrived(end.at[0:mid], at_y + 8 + 4 * j)
        arrived(end.at[mid:], at_y + 9 + 4 * j)
    for place_y, index in ((y, at_x + 1), (below, at_y + 6), (above, at_y + 7), (far, at_y + 14)):
        arrived(unit(columns[1], place_y, 1), index)

    for group, ref, when in finals:
        wait = pltpu.make_async_remote_copy(
            src_ref=ref, dst_ref=ref, send_sem=sem.at[group],
            recv_sem=sem.at[group], device_id=partner, device_id_type=MESH,
        ).wait_send
        if when is None:
            wait()
        else:
            pl.when(when)(wait)
    used = next(semaphores)
    assert used == sem.shape[0], used


def write_out(dq_ref, dk_ref, dv_ref, wg_ref, dq_o, dk_o, dv_o, wg_o, wg_v, sem):
    copies = []
    for u in range(8):
        at = slice(u * ROWS, (u + 1) * ROWS)
        wg_v[at] = wg_ref[u].astype(F32)
        copies.append(pltpu.make_async_copy(wg_v.at[at], wg_o.at[at], sem.at[u]))
        copies[-1].start()
    for i, (src, dst) in enumerate(((dq_ref, dq_o), (dk_ref, dk_o), (dv_ref, dv_o))):
        copies.append(pltpu.make_async_copy(src, dst, sem.at[8 + i]))
        copies[-1].start()
    for copy in copies:
        copy.wait()


def per_device(queries, keys, values, out_grad, out_weight, slopes, counts, gaps):
    width = queries.shape[2]
    nz = lax.axis_size("tensor")
    vmem, hbm = pl.BlockSpec(memory_space=pltpu.VMEM), pl.BlockSpec(memory_space=pltpu.HBM)

    def v(dtype, *shape):
        return pltpu.VMEM(shape, dtype)

    dq, dk, dv, wg = pl.pallas_call(
        kernel,
        out_shape=(
            v(BF16, ROWS, width),
            v(BF16, ROWS, width),
            v(BF16, ROWS, width),
            v(BF16, 8, ROWS, width),
        ),
        in_specs=[vmem, vmem, vmem, hbm, hbm, hbm, hbm, hbm],
        out_specs=(vmem, vmem, vmem, vmem),
        scratch_shapes=[
            v(F32, 8, ROWS),
            v(F32, 8, 8, ROWS),
            v(BF16, 8 * ROWS, ROWS),
            v(BF16, 8 * ROWS, ROWS),
            v(BF16, 4, ROWS, ROWS),
            v(BF16, 4, ROWS, ROWS),
            v(BF16, nz, ROWS, width),
            v(BF16, 4, ROWS, width),
            v(BF16, 2, *out_weight.shape),
            v(F32, 4, ROWS, 8 * ROWS),
            v(BF16, 4, ROWS, ROWS),
            v(BF16, ROWS, width),
            v(BF16, ROWS, width),
            v(BF16, ROWS, width),
            v(F32, ROWS, width),
            v(F32, ROWS, width),
            v(F32, ROWS, width),
            v(BF16, ROWS, width),
            v(BF16, 4, ROWS, ROWS),
            v(F32, 8 * ROWS, ROWS),
            v(F32, 8 * ROWS, ROWS),
            v(BF16, 2, 2, 4, ROWS, ROWS),
            v(BF16, 2, 4, ROWS, ROWS),
            v(BF16, 2, 4, ROWS, ROWS),
            v(F32, 4, 4, 4 * ROWS, ROWS),
            v(BF16, 4, 4, 4 * ROWS, ROWS),
            v(BF16, 4, 2, 2 * ROWS, ROWS),
            v(BF16, 4, 2, 4 * ROWS, ROWS),
            v(F32, 4, 4, ROWS, ROWS),
            v(BF16, 4, 4, ROWS, ROWS),
            v(BF16, 4, 3, ROWS, ROWS),
            pltpu.SemaphoreType.DMA((105,)),
        ],
        compiler_params=pltpu.CompilerParams(
            collective_id=0, has_side_effects=True, vmem_limit_bytes=62 << 20
        ),
        name="block_backward",
    )(
        slopes.reshape(1, -1), counts, gaps,
        queries[0], keys[0], values[0], out_grad[0], out_weight,
    )
    dq, dk, dv, wg = pl.pallas_call(
        write_out,
        out_shape=(
            jax.ShapeDtypeStruct((ROWS, width), BF16),
            jax.ShapeDtypeStruct((ROWS, width), BF16),
            jax.ShapeDtypeStruct((ROWS, width), BF16),
            jax.ShapeDtypeStruct((8 * ROWS, width), F32),
        ),
        in_specs=[vmem] * 4,
        out_specs=(hbm,) * 4,
        scratch_shapes=[
            v(F32, 8 * ROWS, width),
            pltpu.SemaphoreType.DMA((11,)),
        ],
        compiler_params=pltpu.CompilerParams(vmem_limit_bytes=12 << 20),
        name="write_out",
    )(dq, dk, dv, wg)
    return dq[None], dk[None], dv[None], wg


def solution(mesh):
    rows = P("fsdp", "context", "tensor")
    weight = P("fsdp", "tensor")
    placed = (rows, rows, rows, rows, weight, P("tensor"), P("fsdp", "context"))
    return jax.shard_map(
        per_device,
        mesh=mesh,
        in_specs=placed + (P("fsdp", "context"),),
        out_specs=(rows, rows, rows, weight),
        check_vma=False,
    )
```

```python
import itertools

import jax
import jax.numpy as jnp
from jax import lax
from jax.experimental import pallas as pl
from jax.experimental.pallas import tpu as pltpu
from jax.sharding import PartitionSpec as P

MESH = pl.DeviceIdType.MESH
F32, BF16 = jnp.float32, jnp.bfloat16
NEG = -1e30
ROWS = 128
HALF = 256
AXES = (0, 1, 0, 1)
PAIRS = ((0, 1), (2, 3))


def mm(a, b, ca, cb):
    return lax.dot_general(a, b, (((ca,), (cb,)), ((), ())), preferred_element_type=F32)


def kernel(
    slopes_ref, counts_ref, gaps_ref, q_ref, k_ref, v_ref, g_ref, w_ref,
    dq_ref, dk_ref, dv_ref, wg_ref,
    gap_out, gap_all, k_all, v_all, q_head, g_head, g_all, g_far, w_all,
    prob, o_head, o_own, o_masked, o_far, hp_own, hp_out, hp_far, hg_out,
    dq_out, dk_acc, dv_acc, dkv_out, dkv_in, dkv_sum,
    part, part_out, half_in, full_in, part2, part2_out, full2_in,
    sem,
):
    c, z, f = lax.axis_index("context"), lax.axis_index("tensor"), lax.axis_index("fsdp")
    nz = g_all.shape[0]
    y, xl = lax.div(c, 2), lax.rem(c, 2)
    xh, core = lax.div(f, 2), lax.rem(f, 2)
    x = xh * 2 + xl
    place = (x, y)
    side = lax.rem(c + y, 2)
    scaling = ROWS ** (-0.5)
    count = counts_ref[...]
    even = lax.rem(y, 2) == 0

    def dev(c_=None, z_=None, f_=None):
        return {
            "context": c if c_ is None else c_,
            "tensor": z if z_ is None else z_,
            "fsdp": f if f_ is None else f_,
        }

    def beside(axis, step):
        if axis == 0:
            x2 = lax.rem(x + step + 4, 4)
            return dev(c_=y * 2 + lax.rem(x2, 2), f_=lax.div(x2, 2) * 2 + core)
        return dev(c_=lax.rem(y + step + 4, 4) * 2 + xl)

    right, left = dev(z_=lax.rem(z + 1, nz)), dev(z_=lax.rem(z + nz - 1, nz))
    partner = dev(f_=xh * 2 + 1 - core)
    across = dev(c_=y * 2 + 1 - xl, f_=(1 - xh) * 2 + core)

    semaphores = itertools.count()
    finals = []

    def slots(n):
        first = next(semaphores)
        for _ in range(n - 1):
            next(semaphores)
        return first

    def send(src, dst, index, where, group, mine=None):
        copy = pltpu.make_async_remote_copy(
            src_ref=src, dst_ref=dst, send_sem=sem.at[group],
            recv_sem=sem.at[index], device_id=where, device_id_type=MESH,
        )
        if mine is None:
            copy.start()
        else:
            pl.when(jnp.logical_not(mine))(copy.start)

    def give(mine, src, dst, index, where, group):
        send(src, dst, index, where, group, mine)
        pl.when(mine)(pltpu.make_async_copy(src, dst, sem.at[index]).start)

    def arrived(dst, index):
        pltpu.make_async_remote_copy(
            src_ref=dst, dst_ref=dst, send_sem=sem.at[index],
            recv_sem=sem.at[index], device_id=partner, device_id_type=MESH,
        ).wait_recv()

    def at_end(group, ref, when=None):
        finals.append((group, ref, when))

    def cols(ref, head):
        return ref.at[:, pl.ds(pl.multiple_of(head * ROWS, ROWS), ROWS)]

    def rows(ref, shard):
        return ref.at[pl.ds(pl.multiple_of(shard * ROWS, ROWS), ROWS)]

    barrier = pltpu.get_barrier_semaphore()
    greeted = [dev(c_=lax.rem(c + d, 8)) for d in range(1, 8)] + [right, left, partner, across]
    greeted.append(dev(f_=(1 - xh) * 2 + core))
    for where in greeted:
        pl.semaphore_signal(barrier, inc=1, device_id=where, device_id_type=MESH)
    lane8 = lax.broadcasted_iota(jnp.int32, (8, ROWS), 1)
    row8 = lax.broadcasted_iota(jnp.int32, (8, ROWS), 0)
    gap_out[...] = jnp.where(
        lane8 < jnp.broadcast_to(count, (8, ROWS)), jnp.broadcast_to(gaps_ref[...], (8, ROWS)), 0
    ).astype(F32)
    heads = lax.broadcasted_iota(jnp.int32, slopes_ref.shape, 1)
    slope = jnp.sum(jnp.where(heads == y, slopes_ref[...], 0.0), axis=1, keepdims=True)
    pl.semaphore_wait(barrier, len(greeted))

    at_gap, at_kvq, at_ring, at_far, at_w = slots(1), slots(4), slots(2 * nz), slots(1), slots(7)
    by_gap, by_kv, by_q, by_right, by_left, by_far, by_w = (slots(1) for _ in range(7))
    part_rows = ROWS // 2
    hops = nz // 2

    def piece(block, h):
        return g_all.at[block, h * part_rows : (h + 1) * part_rows]

    def to_partner(block, src):
        mine = lax.rem(lax.div(block, 2), 2) == core
        j = 2 * lax.div(block, 4) + lax.rem(block, 2)
        send(src, g_far.at[j], at_far, partner, by_far, mine)

    own_g = pltpu.make_async_copy(g_ref, g_all.at[z], sem.at[at_ring + 2 * nz - 1])
    own_g.start()
    for h in range(2):
        src = g_ref.at[h * part_rows : (h + 1) * part_rows]
        send(src, piece(z, h), at_ring + h, right, by_right)
        send(src, piece(z, h), at_ring + nz + h, left, by_left)
    pltpu.make_async_copy(gap_out, gap_all.at[c], sem.at[at_gap]).start()
    for d in range(1, 8):
        send(gap_out, gap_all.at[c], at_gap, dev(c_=lax.rem(c + d, 8)), by_gap)
    color = lax.rem(xl + y, 2)
    w_half = w_all.shape[1] // 2
    cuts = (0, 192, 384, 512)
    w_next = (beside(1, 1), beside(1, -1), dev(c_=y * 2 + 1 - xl))

    def w_piece(ref, half, i):
        at = pl.multiple_of(half * w_half + cuts[i], 64)
        return ref.at[pl.ds(at, cuts[i + 1] - cuts[i])]

    for i in range(3):
        there = w_piece(w_all.at[xh], 1 - color, i)
        send(w_piece(w_ref, 1 - color, i), there, at_w + i, across, by_w)
    for d in range(8):
        peer = lax.rem(c + d, 8)
        head = lax.div(peer, 2)
        for src, dst in ((k_ref, k_all), (v_ref, v_all)):
            if d == 0:
                pltpu.make_async_copy(cols(src, head), rows(dst, c), sem.at[at_kvq + y]).start()
            else:
                send(cols(src, head), rows(dst, c), at_kvq + y, dev(c_=peer), by_kv)
        if d < 4:
            head = lax.rem(y + d, 4)
            peer = head * 2 + side
            give(peer == c, cols(q_ref, head), q_head.at[y], at_kvq + y, dev(c_=peer), by_q)
    to_partner(z, g_ref)
    own_w = pltpu.make_async_copy(w_ref, w_all.at[xh], sem.at[at_w + 6])
    own_w.start()
    at_end(by_gap, gap_all.at[0:7])
    at_end(by_kv, w_all.at[0, 0:448])
    for by in (by_right, by_left):
        at_end(by, w_all.at[0, 0 : part_rows * (2 * hops - 1)])
    at_end(by_far, g_far)
    at_end(by_w, w_all.at[0])

    def at_end_heads(by):
        at_end(by, o_head.at[0:3], even)
        at_end(by, o_head, jnp.logical_not(even))

    at_end_heads(by_q)

    last = 2 * (hops - 1)

    def ring(k):
        d, h = k // 2 + 1, k % 2
        for way, (where, step, base) in enumerate(
            ((right, nz - d, at_ring), (left, d, at_ring + nz))
        ):
            block = lax.rem(z + step, nz)
            half = way if k == last else h
            arrived(piece(block, half), base + k)
            if d + 1 < hops or (d + 1 == hops and h == way):
                after = min(k + 2, last)
                by = (by_right, by_left)[way]
                send(piece(block, half), piece(block, half), base + after, where, by)
            if h == 1:
                to_partner(block, g_all.at[block])
        if k == last:
            to_partner(lax.rem(z + hops, nz), g_all.at[lax.rem(z + hops, nz)])

    def w_pass(i):
        theirs = w_piece(w_all.at[1 - xh], color, i)
        arrived(theirs, at_w + i)
        send(theirs, theirs, at_w + 3 + i, w_next[i], by_w)

    ring(0)

    arrived(gap_all, at_gap)
    gaps8 = jnp.zeros((8, ROWS), F32)
    before = jnp.zeros((8, ROWS), F32)
    for s in range(8):
        gaps8 = jnp.where(row8 == s, gap_all[s], gaps8)
        before = before + jnp.where(row8 > s, gap_all[s], 0.0)
    r128 = lax.broadcasted_iota(jnp.int32, (ROWS, ROWS), 0)
    l128 = lax.broadcasted_iota(jnp.int32, (ROWS, ROWS), 1)
    upto = (r128 <= l128).astype(BF16)
    offs8 = mm(gaps8.astype(BF16), upto, 1, 0) + jnp.sum(before, axis=1, keepdims=True)
    k_offset = jnp.concatenate([offs8[s : s + 1] for s in range(8)], axis=1)
    k_valid = jnp.concatenate([gaps8[s : s + 1] for s in range(8)], axis=1) > 0.0

    at_o, by_o = slots(1), slots(1)
    at_end_heads(by_o)
    shard = [2 * t + lax.rem(xl + t, 2) for t in range(4)]

    def forward(t):
        n = 2 * ROWS * (t + 1)
        ct = shard[t]
        arrived(k_all.at[0 : 5 * ROWS], at_kvq + t)
        q_gaps = gap_all[ct][0:1]
        q_before = jnp.zeros((1, ROWS), F32)
        for s in range(2 * t + 1):
            q_before = q_before + gap_all[s][0:1] * (s < ct).astype(F32)
        q_offset = jnp.sum(
            jnp.where(l128 <= r128, jnp.broadcast_to(q_gaps, (ROWS, ROWS)), 0.0)
            + jnp.broadcast_to(q_before, (ROWS, ROWS)),
            axis=1, keepdims=True,
        )
        logits = mm(q_head[t], k_all[0:n], 1, 1) * scaling
        logits = logits - slope * (q_offset - k_offset[:, 0:n])
        q_slot = ct * ROWS + lax.broadcasted_iota(jnp.int32, (ROWS, n), 0)
        k_slot = lax.broadcasted_iota(jnp.int32, (ROWS, n), 1)
        allowed = jnp.logical_and(k_valid[:, 0:n], k_slot <= q_slot)
        logits = jnp.where(allowed, logits, NEG)
        peak = jnp.max(logits, axis=1, keepdims=True)
        weight = jnp.where(allowed, jnp.exp(logits - peak), 0.0)
        probs = weight * (1.0 / jnp.sum(weight, axis=1, keepdims=True))
        prob[t, :, 0:n] = probs
        o_head[t] = mm(probs.astype(BF16), v_all[0:n], 1, 0).astype(BF16)
        give(ct == c, o_head.at[t], cols(o_own, y), at_o, dev(c_=ct), by_o)

    ring(1)
    w_pass(0)
    ring(2)
    ring(3)
    ring(4)
    forward(0)
    forward(1)
    ring(5)
    forward(2)
    forward(3)
    w_pass(1)
    w_pass(2)
    ring(6)
    own_g.wait()

    at_of, at_hp, by_of, by_hp = (slots(1) for _ in range(4))
    arrived(o_own, at_o)
    live = lax.broadcasted_iota(jnp.int32, o_own.shape, 0) < jnp.broadcast_to(count, o_own.shape)
    o_masked[...] = jnp.where(live, o_own[...], jnp.zeros_like(o_own))
    send(o_masked, o_far, at_of, partner, by_of)
    at_end(by_of, o_masked)
    arrived(g_far, at_far)

    def both(j):
        mine = g_all[4 * (j // 2) + 2 * core + j % 2]
        return jnp.concatenate([mine, g_far[j]], axis=0)

    class Scatter:
        def __init__(self, axis, terms, out, half, full, by):
            self.axis, self.terms, self.out, self.half, self.full = axis, terms, out, half, full
            self.at, self.by = slots(6), by
            mid = terms.shape[1] // 2
            self.low, self.high = slice(0, mid), slice(mid, 2 * mid)
            p = place[axis]
            self.own = p
            self.far, self.up, self.down = (lax.rem(p + d, 4) for d in (2, 1, 3))
            self.after, self.behind = beside(axis, 1), beside(axis, -1)

        def pass_on(self, group, at, way, more=None):
            terms = self.terms[group, at]
            if more is not None:
                terms = terms + more.astype(F32)
            self.out[group, at] = terms.astype(BF16)
            index = self.at + 2 + 2 * way + (more is not None)
            where = (self.after, self.behind)[way]
            send(self.out.at[group, at], self.full.at[way, at], index, where, self.by)

        def start(self):
            self.out[self.far] = self.terms[self.far].astype(BF16)
            far = self.out.at[self.far]
            send(far.at[self.low], self.half.at[0], self.at, self.after, self.by)
            send(far.at[self.high], self.half.at[1], self.at + 1, self.behind, self.by)

        def more(self):
            self.pass_on(self.up, self.high, 0)
            self.pass_on(self.down, self.low, 1)

        def middle(self):
            arrived(self.half.at[0], self.at)
            self.pass_on(self.up, self.low, 0, self.half[0])
            arrived(self.half.at[1], self.at + 1)
            self.pass_on(self.down, self.high, 1, self.half[1])

        def finish(self):
            for way in range(2):
                arrived(self.full.at[way, self.low], self.at + 2 + 2 * way)
                arrived(self.full.at[way, self.high], self.at + 3 + 2 * way)
            return self.terms[self.own] + self.full[0].astype(F32) + self.full[1].astype(F32)

    arrived(o_far, at_of)
    outputs = jnp.concatenate([o_masked[...], o_far[...]], axis=0)
    for j in range(4):
        product = mm(both(j), outputs, 0, 0)
        for n, axis in enumerate(AXES):
            chunk = product[:, n * ROWS : (n + 1) * ROWS]
            if axis == 0:
                part[n, j] = chunk
            else:
                for i in range(4):
                    part[n, i, j * ROWS : (j + 1) * ROWS] = chunk[i * ROWS : (i + 1) * ROWS]

    class Exchange:
        def __init__(self, axis, terms, out, full, by):
            self.axis, self.terms, self.out, self.full = axis, terms, out, full
            self.at, self.by, self.own = slots(1), by, place[axis]

        def start(self):
            for d in (2, 1, 3):
                group = lax.rem(self.own + d, 4)
                self.out[group] = self.terms[group].astype(BF16)
                where = beside(self.axis, d)
                send(self.out.at[group], self.full.at[d - 1], self.at, where, self.by)

        def finish(self):
            arrived(self.full, self.at)
            return self.terms[self.own] + sum(self.full[d].astype(F32) for d in range(3))

    by_first, by_second = slots(4), slots(1)
    for n in range(4):
        at_end(by_first + n, part_out.at[n, 0:3])
    at_end(by_second, part2_out.at[:, 0:3])
    first, second = [], []
    for n, axis in enumerate(AXES):
        bufs = (part.at[n], part_out.at[n], half_in.at[n], full_in.at[n])
        first.append(Scatter(axis, *bufs, by_first + n))
        bufs = (part2.at[n], part2_out.at[n], full2_in.at[n])
        second.append(Exchange(1 - axis, *bufs, by_second))

    def each(chunks, *calls):
        for call in calls:
            for n in chunks:
                call(n)

    one, two = PAIRS
    each(one, lambda n: first[n].start())
    each(one, lambda n: first[n].more())

    own_w.wait()
    for i in range(3):
        arrived(w_piece(w_all.at[1 - xh], 1 - color, i), at_w + 3 + i)
    width = w_all.shape[2]
    for n in range(0, width, HALF):
        total = jnp.zeros((2 * ROWS, HALF), F32)
        for j in range(4):
            wide = w_all.shape[1] // 2
            w_rows = w_all[j // 2, (j % 2) * wide : (j % 2 + 1) * wide, n : n + HALF]
            total = total + mm(both(j), w_rows, 1, 0)
        hp_own[:, n : n + HALF] = total[0:ROWS]
        hp_out[:, n : n + HALF] = total[ROWS:]
    send(hp_out, hp_far, at_hp, partner, by_hp)
    at_end(by_hp, hp_out)

    arrived(hp_far, at_hp)
    hg_out[...] = jnp.where(live, hp_own[...] + hp_far[...], 0.0).astype(BF16)
    at_g, by_g = slots(1), slots(1)
    at_end_heads(by_g)
    for d in range(4):
        head = lax.rem(y + d, 4)
        peer = head * 2 + side
        give(peer == c, cols(hg_out, head), g_head.at[y], at_g, dev(c_=peer), by_g)

    each(two, lambda n: first[n].start())
    each(one, lambda n: first[n].middle())
    each(two, lambda n: first[n].more())

    def halfway(n):
        part2[n] = first[n].finish().reshape(part2.shape[1:])
        second[n].start()

    held = []
    at_dq, at_dk, at_dv, by_dq, by_dk, by_dv, by_swap = (slots(1) for _ in range(7))
    at_swap = slots(2)
    at_end_heads(by_dq)
    at_end(by_dk, o_head.at[0:3])
    at_end(by_dv, o_head.at[0:3])
    at_end(by_swap, dkv_in)
    arrived(g_head, at_g)
    for t in (3, 2, 1, 0):
        n = 2 * ROWS * (t + 1)
        ct = shard[t]
        grad = g_head[t]
        delta = jnp.sum(grad.astype(F32) * o_head[t].astype(F32), axis=1, keepdims=True)
        probs = prob[t, :, 0:n]
        dprob = mm(grad, v_all[0:n], 1, 1)
        dscore = (probs * (dprob - delta)).astype(BF16)
        dq_out[t] = (mm(dscore, k_all[0:n], 1, 0) * scaling).astype(BF16)
        dk_part = mm(dscore, q_head[t], 0, 0)
        dv_part = mm(probs.astype(BF16), grad, 0, 0)
        if t == 3:
            dk_acc[...] = dk_part
            dv_acc[...] = dv_part
        else:
            dk_acc[0:n] += dk_part
            dv_acc[0:n] += dv_part
        for s in (2 * t + 1, 2 * t):
            at = slice(s * ROWS, (s + 1) * ROWS)
            dkv_out[s % 2, 0, t] = (dk_acc[at] * scaling).astype(BF16)
            dkv_out[s % 2, 1, t] = dv_acc[at].astype(BF16)

    for d in range(4):
        t = lax.rem(y + d, 4)
        held.append((2 * t + lax.rem(xl + t, 2), dq_out.at[t], cols(dq_ref, y), at_dq, by_dq))
    def release(n):
        for _ in range(min(n, len(held))):
            peer, src, dst, index, by = held.pop(0)
            give(peer == c, src, dst, index, dev(c_=peer), by)

    other = dev(c_=y * 2 + 1 - xl)

    def swap(i):
        src = dkv_out.at[1 - xl, i // 2, 2 * (i % 2) : 2 * (i % 2) + 2]
        dst = dkv_in.at[i // 2, 2 * (i % 2) : 2 * (i % 2) + 2]
        send(src, dst, at_swap + i // 2, other, by_swap)


    def add_swapped(i):
        arrived(dkv_in.at[i], at_swap + i)
        for t in range(4):
            at = pl.ds(pl.multiple_of((2 * t + xl) * ROWS, ROWS), ROWS)
            mine = dk_acc[at] * scaling if i == 0 else dv_acc[at]
            dkv_sum[i, t] = (mine + dkv_in[i, t].astype(F32)).astype(BF16)
        dst, index, by = ((dk_ref, at_dk, by_dk), (dv_ref, at_dv, by_dv))[i]
        for d in range(4):
            t = lax.rem(y + d, 4)
            held.append((2 * t + xl, dkv_sum.at[i, t], cols(dst, y), index, by))


    at_x, at_y, by_all = slots(2), slots(16), slots(1)
    at_end(by_all, wg_ref.at[0:7])
    near, back = beside(1, 1), beside(1, -1)
    below, above, far = (lax.rem(y + d, 4) for d in (3, 1, 2))
    columns = (xl * 4, (1 - xl) * 4)
    mid = ROWS // 2

    def unit(column, place_y, i):
        return wg_ref.at[column + place_y, :, i * HALF : (i + 1) * HALF]

    def gather(i):
        mine = unit(columns[0], y, i)
        for n in PAIRS[i]:
            at = slice(n * ROWS, (n + 1) * ROWS)
            wg_ref[columns[0] + y, :, at] = second[n].finish().astype(BF16)
        send(mine, mine, at_x + i, other, by_all)
        send(mine, mine, at_y + 2 * i, near, by_all)
        send(mine, mine, at_y + 2 * i + 1, back, by_all)

    def pass_x(i):
        mine = unit(columns[1], y, i)
        arrived(mine, at_x + i)
        send(mine, mine, at_y + 4 + 2 * i, near, by_all)
        send(mine, mine, at_y + 4 + 2 * i + 1, back, by_all)

    def pass_y(j, i):
        low = unit(columns[j], below, i)
        arrived(low, at_y + 4 * j + 2 * i)
        send(low.at[0:mid], low.at[0:mid], at_y + 8 + 4 * j + 2 * i, near, by_all)
        high = unit(columns[j], above, i)
        arrived(high, at_y + 4 * j + 2 * i + 1)
        send(high.at[mid:], high.at[mid:], at_y + 9 + 4 * j + 2 * i, back, by_all)

    def pass_x_last():
        low = unit(columns[0], below, 1)
        arrived(low, at_y + 2)
        send(low.at[0:mid], low.at[0:mid], at_y + 10, near, by_all)
        send(low, low, at_y + 6, other, by_all)
        high = unit(columns[0], above, 1)
        arrived(high, at_y + 3)
        send(high.at[mid:], high.at[mid:], at_y + 11, back, by_all)
        send(high, high, at_y + 7, other, by_all)

    each(two, lambda n: first[n].middle())
    each(one, halfway)
    swap(0)
    each(two, halfway)
    gather(0)
    swap(1)
    release(2)
    gather(1)
    swap(2)
    release(2)
    pass_x(0)
    swap(3)
    add_swapped(0)
    release(4)
    pass_y(0, 0)
    pass_x_last()
    pass_y(1, 0)
    add_swapped(1)
    release(4)
    end = unit(columns[0], far, 1)
    arrived(end.at[0:mid], at_y + 10)
    arrived(end.at[mid:], at_y + 11)
    send(end, end, at_y + 14, other, by_all)
    arrived(dq_ref, at_dq)
    arrived(dk_ref, at_dk)
    arrived(dv_ref, at_dv)
    for j, column in enumerate(columns):
        end = unit(column, far, 0)
        arrived(end.at[0:mid], at_y + 8 + 4 * j)
        arrived(end.at[mid:], at_y + 9 + 4 * j)
    for place_y, index in ((y, at_x + 1), (below, at_y + 6), (above, at_y + 7), (far, at_y + 14)):
        arrived(unit(columns[1], place_y, 1), index)

    for group, ref, when in finals:
        wait = pltpu.make_async_remote_copy(
            src_ref=ref, dst_ref=ref, send_sem=sem.at[group],
            recv_sem=sem.at[group], device_id=partner, device_id_type=MESH,
        ).wait_send
        if when is None:
            wait()
        else:
            pl.when(when)(wait)
    used = next(semaphores)
    assert used == sem.shape[0], used


def write_out(dq_ref, dk_ref, dv_ref, wg_ref, dq_o, dk_o, dv_o, wg_o, wg_v, sem):
    copies = []
    for i, (src, dst) in enumerate(((dq_ref, dq_o), (dk_ref, dk_o), (dv_ref, dv_o))):
        copies.append(pltpu.make_async_copy(src, dst, sem.at[8 + i]))
        copies[-1].start()
    for u in range(8):
        at = slice(u * ROWS, (u + 1) * ROWS)
        wg_v[at] = wg_ref[u].astype(F32)
        copies.append(pltpu.make_async_copy(wg_v.at[at], wg_o.at[at], sem.at[u]))
        copies[-1].start()
    for copy in copies:
        copy.wait()


def per_device(queries, keys, values, out_grad, out_weight, slopes, counts, gaps):
    width = queries.shape[2]
    nz = lax.axis_size("tensor")
    vmem, hbm = pl.BlockSpec(memory_space=pltpu.VMEM), pl.BlockSpec(memory_space=pltpu.HBM)

    def v(dtype, *shape):
        return pltpu.VMEM(shape, dtype)

    dq, dk, dv, wg = pl.pallas_call(
        kernel,
        out_shape=(
            v(BF16, ROWS, width),
            v(BF16, ROWS, width),
            v(BF16, ROWS, width),
            v(BF16, 8, ROWS, width),
        ),
        in_specs=[vmem, vmem, vmem, hbm, hbm, hbm, hbm, hbm],
        out_specs=(vmem, vmem, vmem, vmem),
        scratch_shapes=[
            v(F32, 8, ROWS),
            v(F32, 8, 8, ROWS),
            v(BF16, 8 * ROWS, ROWS),
            v(BF16, 8 * ROWS, ROWS),
            v(BF16, 4, ROWS, ROWS),
            v(BF16, 4, ROWS, ROWS),
            v(BF16, nz, ROWS, width),
            v(BF16, 4, ROWS, width),
            v(BF16, 2, *out_weight.shape),
            v(F32, 4, ROWS, 8 * ROWS),
            v(BF16, 4, ROWS, ROWS),
            v(BF16, ROWS, width),
            v(BF16, ROWS, width),
            v(BF16, ROWS, width),
            v(F32, ROWS, width),
            v(F32, ROWS, width),
            v(F32, ROWS, width),
            v(BF16, ROWS, width),
            v(BF16, 4, ROWS, ROWS),
            v(F32, 8 * ROWS, ROWS),
            v(F32, 8 * ROWS, ROWS),
            v(BF16, 2, 2, 4, ROWS, ROWS),
            v(BF16, 2, 4, ROWS, ROWS),
            v(BF16, 2, 4, ROWS, ROWS),
            v(F32, 4, 4, 4 * ROWS, ROWS),
            v(BF16, 4, 4, 4 * ROWS, ROWS),
            v(BF16, 4, 2, 2 * ROWS, ROWS),
            v(BF16, 4, 2, 4 * ROWS, ROWS),
            v(F32, 4, 4, ROWS, ROWS),
            v(BF16, 4, 4, ROWS, ROWS),
            v(BF16, 4, 3, ROWS, ROWS),
            pltpu.SemaphoreType.DMA((105,)),
        ],
        compiler_params=pltpu.CompilerParams(
            collective_id=0, has_side_effects=True, vmem_limit_bytes=62 << 20
        ),
        name="block_backward",
    )(
        slopes.reshape(1, -1), counts, gaps,
        queries[0], keys[0], values[0], out_grad[0], out_weight,
    )
    dq, dk, dv, wg = pl.pallas_call(
        write_out,
        out_shape=(
            jax.ShapeDtypeStruct((ROWS, width), BF16),
            jax.ShapeDtypeStruct((ROWS, width), BF16),
            jax.ShapeDtypeStruct((ROWS, width), BF16),
            jax.ShapeDtypeStruct((8 * ROWS, width), F32),
        ),
        in_specs=[vmem] * 4,
        out_specs=(hbm,) * 4,
        scratch_shapes=[
            v(F32, 8 * ROWS, width),
            pltpu.SemaphoreType.DMA((11,)),
        ],
        compiler_params=pltpu.CompilerParams(vmem_limit_bytes=12 << 20),
        name="write_out",
    )(dq, dk, dv, wg)
    return dq[None], dk[None], dv[None], wg


def solution(mesh):
    rows = P("fsdp", "context", "tensor")
    weight = P("fsdp", "tensor")
    placed = (rows, rows, rows, rows, weight, P("tensor"), P("fsdp", "context"))
    return jax.shard_map(
        per_device,
        mesh=mesh,
        in_specs=placed + (P("fsdp", "context"),),
        out_specs=(rows, rows, rows, weight),
        check_vma=False,
    )
```
